32 devices in a mesh: rows: 8 (over z, y), cols: 4 (over x, core).
Axes of the slice: x: 2, y: 2, z: 4, core: 2. Of those that a mesh axis runs over, the one named last changes fastest.
Arguments:
- tiles: bfloat16 [2, 8, 4, 128, 128, 128], P(None, 'rows', 'cols'), may hold values from -0.15625 to 0.15625
- tile_scales: float32 [2, 8, 4, 128], P(None, 'rows', 'cols'), may hold values from 0.5 to 4
- tile_rows: int32 [2, 8, 4, 128], P(None, 'rows', 'cols'), may hold values from 0 to 7
- tile_cols: int32 [2, 8, 4, 128], P(None, 'rows', 'cols'), may hold values from 0 to 1023
- tile_counts: int32 [2, 8, 4], P(None, 'rows', 'cols'), may hold values from 32 to 128, as said below
- labels: int32 [2, 8192], P(None, 'rows'), may hold values from 0 to 31
- learning_rate: float32 [2], replicated, may hold values from 4 to 16
- weights: float32 [32, 524288], P(None, ('cols', 'rows')), may hold values from -6 to 6
Outputs:
- trained: float32 [32, 524288], P(None, ('cols', 'rows'))
- losses: float32 [2, 8192], P(None, ('rows', 'cols'))
The draws below stay inside these ranges and needn't reach their ends.
Inputs may be any that keep to these rules, and one draw needn't show every extreme that they name: Only the first tile_counts[s, r, c] slots of a block are live; in every step some block has all 128 slots live.
All inputs are finite; a program needn't handle non-finite values.
Results may differ from the reference program's by a relative error of at most 0.0021.
Values may be sent and summed in bfloat16 or wider, within the bound.
A program may use at most 128 MiB of HBM per device.

```python
import math
import jax
import jax.numpy as jnp
from jax import lax

CLASS_COUNT = 32
F = 524288
BLK = 128
STEPS = 2
STEP_SAMPLES = 1024
TILES = 128
SAMPLES = 8192
FB_DEV = 1024
RB_DEV = 8
N_ROWS = 8
N_COLS = 4


def draw_tile_counts(key, part):
    shifts = jax.random.randint(key, (STEPS, N_ROWS * N_COLS), 0, 3)
    counts = TILES // jnp.left_shift(jnp.ones_like(shifts), shifts)
    fullest = jax.random.randint(jax.random.fold_in(key, 7), (STEPS, 1), 0, N_ROWS * N_COLS)
    places = jnp.arange(N_ROWS * N_COLS, dtype=jnp.int32)[None, :]
    counts = jnp.where(places == fullest, TILES, counts)
    return counts.reshape(STEPS, N_ROWS, N_COLS).astype(jnp.int32)


def set_ends(entries, rng, smallest, top_value):
    place = [jax.random.randint(jax.random.fold_in(rng, axis), (), 0, length) for axis, length in enumerate(entries.shape)]
    longest = entries.shape.index(max(entries.shape))
    next_to = place[:longest] + [(place[longest] + 1) % entries.shape[longest]] + place[longest + 1:]
    return entries.at[tuple(place)].set(smallest).at[tuple(next_to)].set(top_value)


def levels(rng, shape, pieces, low, top_value):
    gain = 1.0
    for position, shards_of in pieces:
        heights = jax.random.uniform(jax.random.fold_in(jax.random.fold_in(rng, 6), position), (shards_of,), jnp.float32, low / len(pieces), top_value / len(pieces))
        gain = gain * jnp.repeat(jnp.exp(heights), shape[position] // shards_of).reshape((-1,) + (1,) * (len(shape) - 1 - position))
    return gain


def scatter_about(own_key, extent, spread, bound, shards=(), kind=jnp.bfloat16):
    array = jax.random.normal(own_key, extent, jnp.float32) * spread
    if len(shards) > 0:
        array = levels(own_key, extent, shards, -0.22, 0.18) * array
    return jnp.clip(array, min=-bound, max=bound).astype(kind)


def setup_inputs(seed: int = 0) -> dict:
    key_of = jax.random.split(jax.random.key(seed), 9)
    tiles = scatter_about(key_of[0], (STEPS, N_ROWS, N_COLS, TILES, BLK, BLK), ((BLK * BLK * TILES * N_COLS // STEP_SAMPLES) ** -0.5), 0.15625, ((1, 8), (2, 4)))
    tile_scales = jnp.clip(jnp.exp(math.log(4.0) - 2.0794415 * jax.random.uniform(key_of[1], (STEPS, N_ROWS, N_COLS, TILES), jnp.float32) ** levels(key_of[1], (STEPS, N_ROWS, N_COLS, TILES), ((1, 8), (2, 4)), -0.2, 0.2)), 0.5, 4.0)
    tile_rows = set_ends(jax.random.randint(key_of[2], (STEPS, N_ROWS, N_COLS, TILES), 0, RB_DEV), jax.random.fold_in(key_of[2], 1), 0, RB_DEV - 1).astype(jnp.int32)
    tile_cols = set_ends(jax.random.randint(key_of[3], (STEPS, N_ROWS, N_COLS, TILES), 0, FB_DEV), jax.random.fold_in(key_of[3], 1), 0, FB_DEV - 1).astype(jnp.int32)
    tile_counts = draw_tile_counts(jax.random.fold_in(key_of[8], 71), 0)
    labels = set_ends(jax.random.randint(key_of[5], (STEPS, SAMPLES), 0, CLASS_COUNT), jax.random.fold_in(key_of[5], 1), 0, CLASS_COUNT - 1).astype(jnp.int32)
    learning_rate = jnp.clip(jnp.exp(jax.random.uniform(key_of[6], (STEPS,), jnp.float32, math.log(4.0), math.log(16.0))), 4.0, 16.0)
    weights = scatter_about(key_of[7], (CLASS_COUNT, F), 1.5, 6.0, ((1, 32),), jnp.float32)
    return dict(tiles=tiles, tile_scales=tile_scales, tile_rows=tile_rows, tile_cols=tile_cols, tile_counts=tile_counts, labels=labels, learning_rate=learning_rate, weights=weights)


def reference(tiles, tile_scales, tile_rows, tile_cols, tile_counts, labels, learning_rate, weights):
    col_blocks = F // (BLK * N_COLS)
    row_blocks = STEP_SAMPLES // BLK
    slot_ids = jnp.arange(TILES, dtype=jnp.int32)
    block_ids = jnp.arange(row_blocks, dtype=jnp.int32)
    class_ids = jnp.arange(CLASS_COUNT, dtype=jnp.int32)
    col_offsets = (jnp.arange(N_COLS, dtype=jnp.int32) * col_blocks)[:, None]
    current = weights
    losses = []
    for step_index in range(STEPS):
        wide_blocks = current.astype(jnp.bfloat16).reshape(CLASS_COUNT, F // BLK, BLK)

        def one_row(grad_sum, row_index):
            tile_entries = tiles[step_index][row_index].reshape(N_COLS * TILES, BLK, BLK).astype(jnp.float32)
            is_live = slot_ids[None, :] < tile_counts[step_index][row_index][:, None]
            factor = jnp.where(is_live, tile_scales[step_index][row_index], 0.0).reshape(-1)
            col_ids = (tile_cols[step_index][row_index] + col_offsets).reshape(-1).astype(jnp.int32)
            row_ids = tile_rows[step_index][row_index].reshape(-1).astype(jnp.int32)
            selected_entries = jnp.take(wide_blocks, col_ids, axis=1).astype(jnp.float32)
            weighted_products = jnp.einsum("zei,eui->ezu", selected_entries, tile_entries, precision=lax.Precision.HIGHEST)
            row_indicator = (row_ids[:, None] == block_ids[None, :]).astype(jnp.float32) * factor[:, None]
            class_scores = jnp.einsum("iu,idq->duq", row_indicator, weighted_products, precision=lax.Precision.HIGHEST).reshape(CLASS_COUNT, STEP_SAMPLES)
            step_labels = lax.dynamic_slice_in_dim(labels[step_index], (row_index * STEP_SAMPLES).astype(jnp.int32), STEP_SAMPLES)
            exp_logits = jnp.exp(class_scores)
            denominator = jnp.sum(exp_logits, axis=0)
            onehot = (class_ids[:, None] == step_labels[None, :]).astype(jnp.float32)
            sample_loss = jnp.log(denominator) - jnp.sum(onehot * class_scores, axis=0)
            residual = (exp_logits / denominator - onehot).astype(jnp.bfloat16)
            picked_rows = jnp.take(residual.reshape(CLASS_COUNT, row_blocks, BLK), row_ids, axis=1).astype(jnp.float32)
            grad_blocks = jnp.einsum("cts,tsf->ctf", picked_rows, tile_entries, precision=lax.Precision.HIGHEST) * factor[None, :, None]
            grad_sum = grad_sum.at[:, col_ids, :].add(grad_blocks)
            return grad_sum, sample_loss

        grad_sum, row_losses = lax.scan(one_row, jnp.zeros((CLASS_COUNT, F // BLK, BLK), jnp.float32), jnp.arange(N_ROWS, dtype=jnp.int32))
        current = current - learning_rate[step_index] * grad_sum.reshape(CLASS_COUNT, F)
        losses.append(row_losses.reshape(-1))
    return current, jnp.stack(losses)
```

```python
import functools
import math
import jax
import jax.numpy as jnp
from jax import lax
from jax.experimental import pallas as pl
from jax.experimental.pallas import tpu as pltpu
from jax.sharding import PartitionSpec as P

MESH = pl.DeviceIdType.MESH
VMEM_LIMIT = 48 * 1024 * 1024
VM = pl.BlockSpec(memory_space=pltpu.VMEM)
SM = pl.BlockSpec(memory_space=pltpu.SMEM)
LOCAL = pltpu.CompilerParams(vmem_limit_bytes=VMEM_LIMIT)
SLOTS = pltpu.CompilerParams(vmem_limit_bytes=48 * 1024 * 1024)


def lanes(block, size):
    return pl.ds(pl.multiple_of(block * size, size), size)


def pack_body(size, step, capacity, requests_ref, weights_ref, send_ref):
    owners = send_ref.shape[0] // capacity
    full = requests_ref.shape[1] // owners

    @pl.loop(0, capacity)
    def _(index):
        for peer in range(owners):
            where = lanes(requests_ref[step, peer * full + index], size)
            send_ref[peer * capacity + index] = weights_ref[:, where].astype(jnp.bfloat16)


def apply_body(size, step, capacity, requests_ref, rate_ref, weights_ref, grads_ref, out_ref):
    owners = grads_ref.shape[0] // capacity
    full = requests_ref.shape[1] // owners
    out_ref[...] = weights_ref[...]
    rate = rate_ref[step]

    @pl.loop(0, capacity)
    def _(index):
        for peer in range(owners):
            where = lanes(requests_ref[step, peer * full + index], size)
            grad = grads_ref[peer * capacity + index].astype(jnp.float32)
            out_ref[:, where] -= rate * grad


def apply_kernel(size, step, capacity, requests_ref, rate_ref, weights_ref, grads_ref, out_ref):
    apply_body(size, step, capacity, requests_ref, rate_ref, weights_ref, grads_ref, out_ref)


def apply_pack_kernel(
    size, step, capacity, requests_ref, rate_ref, weights_ref, grads_ref, out_ref, send_ref
):
    apply_body(size, step, capacity, requests_ref, rate_ref, weights_ref, grads_ref, out_ref)
    pack_body(size, step + 1, capacity, requests_ref, out_ref, send_ref)


def exchange_kernel(axis, count, send_ref, recv_ref, send_sems, recv_sems, own_sem):
    me = lax.axis_index(axis)
    barrier = pltpu.get_barrier_semaphore()
    for shift in range(1, count):
        peer = lax.rem(me + shift, count)
        pl.semaphore_signal(barrier, inc=1, device_id={axis: peer}, device_id_type=MESH)
    own = pltpu.make_async_copy(send_ref.at[me], recv_ref.at[me], own_sem)
    own.start()
    pl.semaphore_wait(barrier, count - 1)
    copies = []
    for shift in sorted(range(1, count), key=lambda shift: abs(2 * shift - count)):
        peer = lax.rem(me + shift, count)
        copy = pltpu.make_async_remote_copy(
            src_ref=send_ref.at[peer],
            dst_ref=recv_ref.at[me],
            send_sem=send_sems.at[shift],
            recv_sem=recv_sems.at[shift],
            device_id={axis: peer},
            device_id_type=MESH,
        )
        copy.start()
        copies.append(copy)
    own.wait()
    for copy in copies:
        copy.wait()


def exchange(send, axis, count, collective_id):
    return pl.pallas_call(
        functools.partial(exchange_kernel, axis, count),
        out_shape=jax.ShapeDtypeStruct(send.shape, send.dtype),
        in_specs=[VM],
        out_specs=VM,
        scratch_shapes=[
            pltpu.SemaphoreType.DMA((count,)),
            pltpu.SemaphoreType.DMA((count,)),
            pltpu.SemaphoreType.DMA,
        ],
        compiler_params=pltpu.CompilerParams(
            collective_id=collective_id, has_side_effects=True, vmem_limit_bytes=VMEM_LIMIT
        ),
        name="exchange",
    )(send)


def collect_kernel(n_rows, n_cols, mine_ref, all_ref, send_sems, recv_sems, own_sem):
    row, col = lax.axis_index("rows"), lax.axis_index("cols")
    row_peers = [lax.rem(row + shift, n_rows) for shift in range(1, n_rows)]
    col_peers = [lax.rem(col + shift, n_cols) for shift in range(1, n_cols)]
    barrier = pltpu.get_barrier_semaphore()
    for peer in row_peers:
        pl.semaphore_signal(barrier, inc=1, device_id={"rows": peer}, device_id_type=MESH)
    for peer in col_peers:
        pl.semaphore_signal(barrier, inc=1, device_id={"cols": peer}, device_id_type=MESH)
    own = pltpu.make_async_copy(mine_ref, all_ref.at[col, row], own_sem)
    own.start()
    pl.semaphore_wait(barrier, n_rows + n_cols - 2)
    copies = []
    for index, peer in enumerate(row_peers):
        copies.append(
            pltpu.make_async_remote_copy(
                src_ref=mine_ref,
                dst_ref=all_ref.at[col, row],
                send_sem=send_sems.at[index],
                recv_sem=recv_sems.at[index],
                device_id={"rows": peer},
                device_id_type=MESH,
            )
        )
        copies[-1].start()
    own.wait()
    for copy in copies:
        copy.wait()
    copies = []
    for index, peer in enumerate(col_peers):
        copies.append(
            pltpu.make_async_remote_copy(
                src_ref=all_ref.at[col],
                dst_ref=all_ref.at[col],
                send_sem=send_sems.at[n_rows + index],
                recv_sem=recv_sems.at[n_rows + index],
                device_id={"cols": peer},
                device_id_type=MESH,
            )
        )
        copies[-1].start()
    for copy in copies:
        copy.wait()


def collect(mine, n_rows, n_cols):
    return pl.pallas_call(
        functools.partial(collect_kernel, n_rows, n_cols),
        out_shape=jax.ShapeDtypeStruct((n_cols, n_rows, *mine.shape), mine.dtype),
        in_specs=[VM],
        out_specs=VM,
        scratch_shapes=[
            pltpu.SemaphoreType.DMA((n_rows + n_cols,)),
            pltpu.SemaphoreType.DMA((n_rows + n_cols,)),
            pltpu.SemaphoreType.DMA,
        ],
        compiler_params=pltpu.CompilerParams(collective_id=0, has_side_effects=True),
        name="collect",
    )(mine)


GROUP = 16


def slot_scalars(step, place_of, slot, code_ref, row_ref, scale_ref, count_ref):
    place = place_of(code_ref[step, slot])
    factor = jnp.where(slot < count_ref[step, 0, 0], scale_ref[step, 0, 0, slot], 0.0)
    return place, row_ref[step, 0, 0, slot], factor


def fetch_tiles(step, tiles_ref, held_ref, sems):
    def copy(group):
        part = pl.ds(group * GROUP, GROUP)
        return pltpu.make_async_copy(
            tiles_ref.at[step, 0, 0, part], held_ref.at[part], sems.at[group]
        )

    for group in range(held_ref.shape[0] // GROUP):
        copy(group).start()
    return lambda group: copy(group).wait()


def scores_kernel(
    step, place_of, code_ref, row_ref, scale_ref, count_ref, recv_ref, tiles_ref, out_ref,
    held_ref, sems,
):
    size = held_ref.shape[-1]
    arrived = fetch_tiles(step, tiles_ref, held_ref, sems)
    out_ref[...] = jnp.zeros_like(out_ref)

    @pl.loop(0, held_ref.shape[0] // GROUP)
    def _(group):
        arrived(group)
        products = []
        for lane in range(GROUP):
            slot = group * GROUP + lane
            place, row, factor = slot_scalars(
                step, place_of, slot, code_ref, row_ref, scale_ref, count_ref
            )
            product = lax.dot_general(
                recv_ref[place],
                held_ref[slot],
                (((1,), (1,)), ((), ())),
                preferred_element_type=jnp.float32,
            )
            products.append((row, product * factor))
        for row, product in products:
            out_ref[:, lanes(row, size)] += product


def classify_kernel(
    axis, count, step, part_ref, labels_ref, residual_ref, loss_ref, held, losses, send_sems,
    recv_sems,
):
    me = lax.axis_index(axis)
    barrier = pltpu.get_barrier_semaphore()
    for shift in range(1, count):
        peer = lax.rem(me + shift, count)
        pl.semaphore_signal(barrier, inc=1, device_id={axis: peer}, device_id_type=MESH)
    pl.semaphore_wait(barrier, count - 1)
    copies = []
    for shift in range(1, count):
        peer = lax.rem(me + shift, count)
        copy = pltpu.make_async_remote_copy(
            src_ref=part_ref,
            dst_ref=held.at[shift],
            send_sem=send_sems.at[shift],
            recv_sem=recv_sems.at[shift],
            device_id={axis: peer},
            device_id_type=MESH,
        )
        copy.start()
        copies.append(copy)
    scores = part_ref[...]
    for shift, copy in enumerate(copies):
        copy.wait()
        scores = scores + held[shift + 1]
    exp_scores = jnp.exp(scores)
    total = jnp.sum(exp_scores, axis=0, keepdims=True)
    class_ids = lax.broadcasted_iota(jnp.int32, scores.shape, 0)
    onehot = (class_ids == labels_ref[step : step + 1, :]).astype(jnp.float32)
    losses[...] = jnp.log(total) - jnp.sum(onehot * scores, axis=0, keepdims=True)
    if loss_ref.shape == losses.shape:
        loss_ref[...] = losses[...]
    else:
        loss_ref[...] = losses[:, lanes(me, loss_ref.shape[1])]
    residual_ref[...] = (exp_scores / total - onehot).astype(jnp.bfloat16)


def classify(step, n_cols, part, labels):
    classes, samples = part.shape
    owned = samples // n_cols
    return pl.pallas_call(
        functools.partial(classify_kernel, "cols", n_cols, step),
        out_shape=(
            jax.ShapeDtypeStruct((classes, samples), jnp.bfloat16),
            jax.ShapeDtypeStruct((1, owned if owned % 128 == 0 else samples), jnp.float32),
        ),
        in_specs=[VM, VM],
        out_specs=(VM, VM),
        scratch_shapes=[
            pltpu.VMEM((n_cols, classes, samples), jnp.float32),
            pltpu.VMEM((1, samples), jnp.float32),
            pltpu.SemaphoreType.DMA((n_cols,)),
            pltpu.SemaphoreType.DMA((n_cols,)),
        ],
        compiler_params=pltpu.CompilerParams(collective_id=1 + step, has_side_effects=True),
        name="classify",
    )(part, labels)


def grads_kernel(
    step, place_of, code_ref, row_ref, scale_ref, count_ref, residual_ref, tiles_ref,
    out_ref, total, held_ref, sems,
):
    size = held_ref.shape[-1]
    arrived = fetch_tiles(step, tiles_ref, held_ref, sems)
    total[...] = jnp.zeros_like(total)

    @pl.loop(0, held_ref.shape[0] // GROUP)
    def _(group):
        arrived(group)
        products = []
        for lane in range(GROUP):
            slot = group * GROUP + lane
            place, row, factor = slot_scalars(
                step, place_of, slot, code_ref, row_ref, scale_ref, count_ref
            )
            product = jnp.dot(
                residual_ref[:, lanes(row, size)],
                held_ref[slot],
                preferred_element_type=jnp.float32,
            )
            products.append((place, product * factor))
        for place, product in products:
            total[place] += product

    out_ref[...] = total[...].astype(jnp.bfloat16)


def sparse_program(
    capacity, branch, code, requests,
    tiles, tile_scales, tile_rows, tile_cols, tile_counts, labels, learning_rate, weights
):
    classes = weights.shape[0]
    size = tiles.shape[-1]
    steps = tiles.shape[0]
    n_rows, n_cols = lax.axis_size("rows"), lax.axis_size("cols")
    full = requests.shape[1] // n_rows
    samples = labels.shape[1]
    entries = n_rows * capacity
    packed = jax.ShapeDtypeStruct((entries, classes, size), jnp.bfloat16)
    owned = samples // n_cols
    scalars = (code, tile_rows, tile_scales, tile_counts)
    trade_id = 1 + steps + branch
    slots = tiles.shape[3]
    in_hbm = pl.BlockSpec(memory_space=pltpu.HBM)
    tile_room = [pltpu.VMEM(tiles.shape[3:], tiles.dtype), pltpu.SemaphoreType.DMA((slots // GROUP,))]

    def place_of(x):
        return x // full * capacity + lax.rem(x, full)

    def trade(x):
        blocks = x.reshape(n_rows, capacity, classes, size)
        return exchange(blocks, "rows", n_rows, trade_id).reshape(packed.shape)

    current = weights
    send = pl.pallas_call(
        functools.partial(pack_body, size, 0, capacity),
        out_shape=packed, in_specs=[SM, VM], out_specs=VM, compiler_params=LOCAL, name="pack",
    )(requests, current)
    losses = []
    for step in range(steps):
        got = trade(send)
        part = pl.pallas_call(
            functools.partial(scores_kernel, step, place_of),
            out_shape=jax.ShapeDtypeStruct((classes, samples), jnp.float32),
            in_specs=[SM] * 4 + [VM, in_hbm], out_specs=VM, compiler_params=SLOTS,
            scratch_shapes=tile_room, name="scores",
        )(*scalars, got, tiles)
        residual, loss = classify(step, n_cols, part, labels)
        if owned % 128 != 0:
            start = lax.axis_index("cols") * owned
            loss = lax.dynamic_slice_in_dim(loss, start, owned, axis=1)
        losses.append(loss)
        grads = pl.pallas_call(
            functools.partial(grads_kernel, step, place_of),
            out_shape=packed,
            in_specs=[SM] * 4 + [VM, in_hbm], out_specs=VM, compiler_params=SLOTS,
            scratch_shapes=[pltpu.VMEM((entries, classes, size), jnp.float32), *tile_room],
            name="grads",
        )(*scalars, residual, tiles)
        grads = trade(grads)
        shape = jax.ShapeDtypeStruct(current.shape, current.dtype)
        more = step + 1 < steps
        current, *send = pl.pallas_call(
            functools.partial(apply_pack_kernel if more else apply_kernel, size, step, capacity),
            out_shape=(shape, packed) if more else (shape,),
            in_specs=[SM, SM, VM, VM], out_specs=(VM, VM) if more else (VM,),
            compiler_params=LOCAL, name="apply",
        )(requests, learning_rate, current, grads)
        send = send[0] if more else None
    return current, jnp.concatenate(losses)


def per_device(
    tiles, tile_scales, tile_rows, tile_cols, tile_counts, labels, learning_rate, weights
):
    args = (tiles, tile_scales, tile_rows, tile_cols, tile_counts, labels, learning_rate, weights)
    size, slots = tiles.shape[-1], tiles.shape[3]
    n_rows, n_cols = lax.axis_size("rows"), lax.axis_size("cols")
    per_owner = weights.shape[1] // size
    full = min(per_owner, slots)
    mean = slots / n_rows
    tiers = [math.ceil(mean + spread * math.sqrt(mean)) for spread in (1.75, 2, 2.25, 2.5, 3, 4)]
    tiers = sorted({min(tier, full) for tier in tiers} | {full})
    slot_ids = jnp.arange(slots, dtype=jnp.int32)

    live = slot_ids < tile_counts[:, 0, 0, None]
    mine = jnp.where(live, tile_cols[:, 0, 0], -1)
    owner = jnp.where(live, mine // per_owner, -1)
    same = mine[:, :, None] == mine[:, None, :]
    before = slot_ids[:, None] > slot_ids[None, :]
    fresh = live & ~jnp.any(same & before, axis=-1)
    lower = (owner[:, :, None] == owner[:, None, :]) & (mine[:, None, :] < mine[:, :, None])
    rank = jnp.sum((lower & fresh[:, None, :]).astype(jnp.int32), axis=-1)
    code = jnp.where(live, owner * full + rank, 0)
    everyone = collect(jnp.where(fresh, mine * full + rank, -1), n_rows, n_cols)
    most = jnp.max(jnp.where(everyone >= 0, everyone % full, 0)) + 1

    row, col = lax.axis_index("rows"), lax.axis_index("cols")
    peers = lax.dynamic_index_in_dim(everyone, col, 0, keepdims=False)
    local = peers // full - row * per_owner
    asked = (peers >= 0) & (local >= 0) & (local < per_owner)
    order = jnp.where(asked, peers % full, -1)
    picks = order[..., None, :] == jnp.arange(full, dtype=jnp.int32)[:, None]
    wanted = jnp.sum(jnp.where(picks, local[..., None, :], 0), axis=-1)
    requests = jnp.swapaxes(wanted, 0, 1).reshape(-1, n_rows * full)

    def at_capacity(capacity, branch):
        return functools.partial(sparse_program, capacity, branch)

    branches = [at_capacity(capacity, branch) for branch, capacity in enumerate(tiers)]
    operands = (code, requests, *args)
    if len(branches) == 1:
        return branches[0](*operands)
    chosen = sum((most > tier).astype(jnp.int32) for tier in tiers[:-1])
    return lax.switch(chosen, branches, *operands)


SPILL = 12
TIERS = ((23, 14), (24, 16), (26, 18), (28, 22))
LEFT_RIGHT = (((1,), (1,)), ((), ()))


def teams(n_rows):
    team = n_rows // 2
    row = lax.axis_index("rows")
    half, place = row // team, lax.rem(row, team)
    mate = lambda shift: half * team + lax.rem(place + shift, team)
    other = lambda shift: (1 - half) * team + lax.rem(place + shift, team)
    return team, row, half, place, mate, other


def greet_rows(peers):
    barrier = pltpu.get_barrier_semaphore()
    for peer in peers:
        pl.semaphore_signal(barrier, inc=1, device_id={"rows": peer}, device_id_type=MESH)
    return lambda: pl.semaphore_wait(barrier, len(peers))


def slots_of(tile_cols, count, steps):
    slots = tile_cols.shape[1]
    ids = lax.broadcasted_iota(jnp.int32, (1, slots), 1)
    return [(tile_cols[s : s + 1, :], ids < count(s)) for s in range(steps)]


def mark_kernel(n_rows, n_cols, steps, cols_ref, count_ref, all_ref, mine, send_sems, recv_sems, own_sem):
    row, col = lax.axis_index("rows"), lax.axis_index("cols")
    row_peers = [lax.rem(row + shift, n_rows) for shift in range(1, n_rows)]
    col_peers = [lax.rem(col + shift, n_cols) for shift in range(1, n_cols)]
    barrier = pltpu.get_barrier_semaphore()
    for peer in row_peers:
        pl.semaphore_signal(barrier, inc=1, device_id={"rows": peer}, device_id_type=MESH)
    for peer in col_peers:
        pl.semaphore_signal(barrier, inc=1, device_id={"cols": peer}, device_id_type=MESH)
    size = mine.shape[1]
    marks = []
    for cols, live in slots_of(cols_ref[...], lambda s: count_ref[s, 0, 0], steps):
        slots = cols.shape[1]
        owners = lax.broadcasted_iota(jnp.int32, (n_rows, slots), 0)
        places = lax.broadcasted_iota(jnp.int32, (size, slots), 0)
        first = jnp.where(live & (cols >> 7 == owners), 1.0, 0.0).astype(jnp.bfloat16)
        second = jnp.where((cols & 127) == places, 1.0, 0.0).astype(jnp.bfloat16)
        count = lax.dot_general(first, second, LEFT_RIGHT, preferred_element_type=jnp.float32)
        marks.append(jnp.minimum(count, 1.0))
    mine[...] = jnp.concatenate(marks, axis=0).astype(jnp.bfloat16)
    pl.semaphore_wait(barrier, n_rows + n_cols - 2)
    own = pltpu.make_async_copy(mine, all_ref.at[col, row], own_sem)
    own.start()
    copies = []
    for index, peer in enumerate(row_peers):
        copies.append(
            pltpu.make_async_remote_copy(
                src_ref=mine,
                dst_ref=all_ref.at[col, row],
                send_sem=send_sems.at[index],
                recv_sem=recv_sems.at[index],
                device_id={"rows": peer},
                device_id_type=MESH,
            )
        )
        copies[-1].start()
    own.wait()
    for copy in copies:
        copy.wait()
    copies = []
    for index, peer in enumerate(col_peers):
        copies.append(
            pltpu.make_async_remote_copy(
                src_ref=all_ref.at[col],
                dst_ref=all_ref.at[col],
                send_sem=send_sems.at[n_rows + index],
                recv_sem=recv_sems.at[n_rows + index],
                device_id={"cols": peer},
                device_id_type=MESH,
            )
        )
        copies[-1].start()
    for copy in copies:
        copy.wait()


def mark(tile_cols, tile_counts, n_rows, n_cols, size):
    steps = tile_cols.shape[0]
    return pl.pallas_call(
        functools.partial(mark_kernel, n_rows, n_cols, steps),
        out_shape=jax.ShapeDtypeStruct((n_cols, n_rows, steps * n_rows, size), jnp.bfloat16),
        in_specs=[VM, SM],
        out_specs=VM,
        scratch_shapes=[
            pltpu.VMEM((steps * n_rows, size), jnp.bfloat16),
            pltpu.SemaphoreType.DMA((n_rows + n_cols,)),
            pltpu.SemaphoreType.DMA((n_rows + n_cols,)),
            pltpu.SemaphoreType.DMA,
        ],
        compiler_params=pltpu.CompilerParams(collective_id=0, has_side_effects=True),
        name="mark",
    )(tile_cols, tile_counts)


def plan_kernel(
    n_rows, steps, all_ref, cols_ref, count_ref, code_ref, list_ref, tier_ref, keys, shared_keys, table
):
    team, row, half, _, _, _ = teams(n_rows)
    col = lax.axis_index("cols")
    size = all_ref.shape[-1]
    n_cols = all_ref.shape[0]
    depth = steps * n_rows
    before = lax.broadcasted_iota(jnp.int32, (size, size), 0)
    after = lax.broadcasted_iota(jnp.int32, (size, size), 1)
    triangle = jnp.where(before < after, 1.0, 0.0).astype(jnp.bfloat16)

    def ranks(flags):
        flat = flags.reshape(-1, size).astype(jnp.bfloat16)
        return jnp.dot(flat, triangle, preferred_element_type=jnp.float32).reshape(flags.shape)

    owner = lax.rem(lax.broadcasted_iota(jnp.int32, (1, depth, size), 1), n_rows)
    most_listed, most_shared = [], []
    for part in range(2):
        needs = all_ref[:, part * team : (part + 1) * team].astype(jnp.float32)
        near = owner // team == part
        wanted = needs[:, 0]
        for index in range(1, team):
            wanted = wanted + needs[:, index]
        alone = near | (wanted < 1.5)
        listed = jnp.where(alone[:, None], needs, 0.0)
        rank = ranks(listed)
        over = jnp.where(rank >= SPILL, listed, 0.0)
        spilled = over[:, 0]
        for index in range(1, team):
            spilled = jnp.maximum(spilled, over[:, index])
        shared = jnp.where(near | ((wanted < 1.5) & (spilled < 0.5)), 0.0, 1.0)
        shared_rank = ranks(shared)
        keep = (listed > 0.5) & (near[:, None] | (rank < SPILL))
        keys[:, part * team : (part + 1) * team] = jnp.where(keep, rank, -1.0)
        shared_keys[:, part] = jnp.where(shared > 0.5, shared_rank, -1.0)
        most_listed.append(jnp.max(jnp.where(keep & near[:, None], rank, -1.0)))
        most_shared.append(jnp.max(jnp.where(shared > 0.5, shared_rank, -1.0)))
    listed = jnp.maximum(*most_listed) + 1.0
    shared = jnp.maximum(*most_shared) + 1.0
    tier = jnp.int32(0)
    for cap, shared_cap in TIERS:
        tier = tier + jnp.where((listed > cap) | (shared > shared_cap), 1, 0).astype(jnp.int32)
    tier_ref[0] = tier

    table[...] = jnp.full_like(table, -1.0)
    sub = lax.broadcasted_iota(jnp.int32, (n_rows, size), 0)
    slot = lax.rem(sub, team)
    n_lists = 2 * team + 1
    for s in range(steps):
        mine = pl.ds(s * n_rows + row, 1)
        for index in range(team):
            at = 2 * n_rows * s + index
            table[at : at + 1, :] = keys[col, half * team + index, mine, :]
            table[at + team : at + team + 1, :] = keys[col, (1 - half) * team + index, mine, :]
        at = 2 * n_rows * s + 2 * team
        table[at : at + 1, :] = shared_keys[col, 1 - half, mine, :]
        block = pl.ds(s * n_rows, n_rows)
        listed_key = keys[col, row, block, :]
        shared_key = shared_keys[col, half, block, :]
        kind = jnp.where(sub // team == half, slot, team + slot)
        value = (kind * size).astype(jnp.float32) + listed_key
        other = ((2 * team + slot) * size).astype(jnp.float32) + shared_key
        at = 2 * n_rows * steps + s * n_rows
        table[at : at + n_rows, :] = jnp.where(shared_key >= 0.0, other, value)
    flipped = table[...].T
    lane = after.astype(jnp.float32)
    down = before.astype(jnp.float32)
    for s in range(steps):
        for index in range(n_lists):
            at = 2 * n_rows * s + index
            hit = flipped[:, at : at + 1] == lane
            picked = jnp.sum(jnp.where(hit, down, 0.0), axis=0, keepdims=True)
            list_ref[s : s + 1, index * size : (index + 1) * size] = picked.astype(jnp.int32)
    for s, (cols, live) in enumerate(slots_of(cols_ref[...], lambda s: count_ref[s, 0, 0], steps)):
        chosen = jnp.zeros((size, size), jnp.float32)
        for index in range(n_rows):
            at = 2 * n_rows * steps + s * n_rows + index
            chosen = jnp.where(cols >> 7 == index, flipped[:, at : at + 1], chosen)
        code = jnp.sum(jnp.where((cols & 127) == before, chosen, 0.0), axis=0, keepdims=True)
        code_ref[s : s + 1, :] = jnp.where(live, code, 0.0).astype(jnp.int32)


def plan(everyone, tile_cols, tile_counts, n_rows):
    steps, slots = tile_cols.shape
    size = everyone.shape[-1]
    lists = n_rows + 1
    return pl.pallas_call(
        functools.partial(plan_kernel, n_rows, steps),
        out_shape=(
            jax.ShapeDtypeStruct((steps, slots), jnp.int32),
            jax.ShapeDtypeStruct((steps, lists * size), jnp.int32),
            jax.ShapeDtypeStruct((1,), jnp.int32),
        ),
        in_specs=[VM, VM, SM],
        out_specs=(VM, VM, SM),
        scratch_shapes=[
            pltpu.VMEM(everyone.shape, jnp.float32),
            pltpu.VMEM((everyone.shape[0], 2, *everyone.shape[2:]), jnp.float32),
            pltpu.VMEM((size, size), jnp.float32),
        ],
        compiler_params=LOCAL,
        name="plan",
    )(everyone, tile_cols, tile_counts)


class Room:
    def __init__(self, team, listed, shared):
        self.team, self.listed, self.shared = team, listed, shared
        self.spill = team * listed
        self.common = self.spill + team * SPILL
        self.packed = self.common + shared
        self.spread = self.common + team * shared

    def near(self, index):
        return pl.ds(index * self.listed, self.listed)

    def far(self, index):
        return pl.ds(self.spill + index * SPILL, SPILL)

    def group(self, index):
        return pl.ds(self.common + index * self.shared, self.shared)

    def place(self, code, size):
        kind, rank = code // size, lax.rem(code, size)
        far = self.spill + (kind - self.team) * SPILL
        common = self.common + (kind - 2 * self.team) * self.shared
        base = jnp.where(kind < 2 * self.team, far, common)
        return jnp.where(kind < self.team, kind * self.listed, base) + rank

    def entries(self, body):
        def run(first, lists, count, start):
            @pl.loop(0, count)
            def _(index):
                for which in range(lists):
                    body(start + which * count + index, first + which, index)

        run(0, self.team, self.listed, 0)
        run(self.team, self.team, SPILL, self.spill)
        run(2 * self.team, 1, self.shared, self.common)


def pack_lists(room, step, lists_ref, weights_ref, send_ref):
    size = send_ref.shape[-1]

    def body(entry, which, index):
        where = lanes(lists_ref[step, which * size + index], size)
        send_ref[entry] = weights_ref[:, where].astype(jnp.bfloat16)

    room.entries(body)


def apply_lists(room, step, lists_ref, rate_ref, weights_ref, grads_ref, out_ref):
    size = grads_ref.shape[-1]
    out_ref[...] = weights_ref[...]
    rate = rate_ref[step]

    def body(entry, which, index):
        where = lanes(lists_ref[step, which * size + index], size)
        out_ref[:, where] -= rate * grads_ref[entry].astype(jnp.float32)

    room.entries(body)


def apply_pack_lists(room, step, lists_ref, rate_ref, weights_ref, grads_ref, out_ref, send_ref):
    apply_lists(room, step, lists_ref, rate_ref, weights_ref, grads_ref, out_ref)
    pack_lists(room, step + 1, lists_ref, out_ref, send_ref)


def row_copy(sems, index, src, dst, peer):
    return pltpu.make_async_remote_copy(
        src_ref=src,
        dst_ref=dst,
        send_sem=sems[0].at[index],
        recv_sem=sems[1].at[index],
        device_id={"rows": peer},
        device_id_type=MESH,
    )


def spread_kernel(room, n_rows, send_ref, got_ref, send_sems, recv_sems, own_sem):
    team, _, _, place, mate, other = teams(n_rows)
    sems = (send_sems, recv_sems)
    shifts = range(1, team)
    entered = greet_rows([mate(s) for s in shifts] + [other(s) for s in range(team)])
    own = pltpu.make_async_copy(send_ref.at[room.near(place)], got_ref.at[room.near(place)], own_sem)
    own.start()
    entered()
    common = pl.ds(room.common, room.shared)
    group = row_copy(sems, 0, send_ref.at[common], got_ref.at[room.group(place)], other(0))
    group.start()
    copies = []
    for shift in range(team):
        to = lax.rem(place + shift, team)
        copies.append(row_copy(
            sems, 1 + shift, send_ref.at[room.far(to)], got_ref.at[room.far(place)], other(shift)
        ))
        copies[-1].start()
    for shift in shifts:
        to = lax.rem(place + shift, team)
        copies.append(row_copy(
            sems, team + shift, send_ref.at[room.near(to)], got_ref.at[room.near(place)], mate(shift)
        ))
        copies[-1].start()
    group.wait_recv()
    for shift in shifts:
        mine = room.group(place)
        copies.append(row_copy(
            sems, 2 * team - 1 + shift, got_ref.at[mine], got_ref.at[mine], mate(shift)
        ))
        copies[-1].start()
    group.wait_send()
    own.wait()
    for copy in copies:
        copy.wait()


def gather_kernel(room, n_rows, grads_ref, out_ref, pool, total, send_sems, recv_sems, own_sem):
    team, _, _, place, mate, other = teams(n_rows)
    sems = (send_sems, recv_sems)
    shifts = range(1, team)
    entered = greet_rows([mate(s) for s in shifts] + [other(s) for s in range(team)])
    own = pltpu.make_async_copy(grads_ref.at[room.near(place)], out_ref.at[room.near(place)], own_sem)
    own.start()
    entered()
    pools, copies = [], []
    for shift in shifts:
        to = lax.rem(place + shift, team)
        pools.append(row_copy(
            sems, shift, grads_ref.at[room.group(to)], pool.at[shift - 1], mate(shift)
        ))
        pools[-1].start()
    for shift in range(team):
        to = lax.rem(place + shift, team)
        copies.append(row_copy(
            sems, team + shift, grads_ref.at[room.far(to)], out_ref.at[room.far(place)], other(shift)
        ))
        copies[-1].start()
    for shift in shifts:
        to = lax.rem(place + shift, team)
        copies.append(row_copy(
            sems, 2 * team - 1 + shift, grads_ref.at[room.near(to)], out_ref.at[room.near(place)],
            mate(shift),
        ))
        copies[-1].start()
    for copy in pools:
        copy.wait_recv()

    mine = room.common + place * room.shared

    @pl.loop(0, room.shared)
    def _(index):
        value = grads_ref[mine + index].astype(jnp.float32)
        for part in range(team - 1):
            value = value + pool[part, index].astype(jnp.float32)
        total[index] = value.astype(jnp.bfloat16)

    common = pl.ds(room.common, room.shared)
    group = row_copy(sems, 0, total, out_ref.at[common], other(0))
    group.start()
    for copy in pools:
        copy.wait_send()
    own.wait()
    for copy in copies:
        copy.wait()
    group.wait()


def remote_sems(count):
    return [pltpu.SemaphoreType.DMA((count,)), pltpu.SemaphoreType.DMA((count,)), pltpu.SemaphoreType.DMA]


def team_program(
    n_rows, listed, shared, branch, code, lists,
    tiles, tile_scales, tile_rows, tile_cols, tile_counts, labels, learning_rate, weights
):
    classes = weights.shape[0]
    size = tiles.shape[-1]
    steps, slots = tiles.shape[0], tiles.shape[3]
    n_cols = lax.axis_size("cols")
    samples = labels.shape[1]
    owned = samples // n_cols
    room = Room(n_rows // 2, listed, shared)
    packed = jax.ShapeDtypeStruct((room.packed, classes, size), jnp.bfloat16)
    spread = jax.ShapeDtypeStruct((room.spread, classes, size), jnp.bfloat16)
    scalars = (code, tile_rows, tile_scales, tile_counts)
    in_hbm = pl.BlockSpec(memory_space=pltpu.HBM)
    tile_room = [pltpu.VMEM(tiles.shape[3:], tiles.dtype), pltpu.SemaphoreType.DMA((slots // GROUP,))]

    def remote(index):
        return pltpu.CompilerParams(
            collective_id=1 + steps + 2 * branch + index, has_side_effects=True,
            vmem_limit_bytes=VMEM_LIMIT,
        )

    current = weights
    send = pl.pallas_call(
        functools.partial(pack_lists, room, 0),
        out_shape=packed, in_specs=[SM, VM], out_specs=VM, compiler_params=LOCAL, name="pack",
    )(lists, current)
    losses = []
    for step in range(steps):
        got = pl.pallas_call(
            functools.partial(spread_kernel, room, n_rows),
            out_shape=spread, in_specs=[VM], out_specs=VM, compiler_params=remote(0),
            scratch_shapes=remote_sems(3 * room.team - 1), name="spread",
        )(send)
        part = pl.pallas_call(
            functools.partial(scores_kernel, step, lambda x: room.place(x, size)),
            out_shape=jax.ShapeDtypeStruct((classes, samples), jnp.float32),
            in_specs=[SM] * 4 + [VM, in_hbm], out_specs=VM, compiler_params=SLOTS,
            scratch_shapes=tile_room, name="scores",
        )(*scalars, got, tiles)
        residual, loss = classify(step, n_cols, part, labels)
        losses.append(loss)
        grads = pl.pallas_call(
            functools.partial(grads_kernel, step, lambda x: room.place(x, size)),
            out_shape=spread,
            in_specs=[SM] * 4 + [VM, in_hbm], out_specs=VM, compiler_params=SLOTS,
            scratch_shapes=[pltpu.VMEM((room.spread, classes, size), jnp.float32), *tile_room],
            name="grads",
        )(*scalars, residual, tiles)
        grads = pl.pallas_call(
            functools.partial(gather_kernel, room, n_rows),
            out_shape=packed, in_specs=[VM], out_specs=VM, compiler_params=remote(1),
            scratch_shapes=[
                pltpu.VMEM((room.team - 1, shared, classes, size), jnp.bfloat16),
                pltpu.VMEM((shared, classes, size), jnp.bfloat16),
                *remote_sems(3 * room.team - 1),
            ],
            name="gather",
        )(grads)
        shape = jax.ShapeDtypeStruct(current.shape, current.dtype)
        more = step + 1 < steps
        current, *send = pl.pallas_call(
            functools.partial(apply_pack_lists if more else apply_lists, room, step),
            out_shape=(shape, packed) if more else (shape,),
            in_specs=[SM, SM, VM, VM], out_specs=(VM, VM) if more else (VM,),
            compiler_params=LOCAL, name="apply",
        )(lists, learning_rate, current, grads)
        send = send[0] if more else None
    return current, jnp.concatenate(losses)


def team_device(
    tiles, tile_scales, tile_rows, tile_cols, tile_counts, labels, learning_rate, weights
):
    args = (tiles, tile_scales, tile_rows, tile_cols, tile_counts, labels, learning_rate, weights)
    size = tiles.shape[-1]
    n_rows, n_cols = lax.axis_size("rows"), lax.axis_size("cols")
    cols = tile_cols[:, 0, 0]
    everyone = mark(cols, tile_counts, n_rows, n_cols, size)
    code, lists, tier = plan(everyone, cols, tile_counts, n_rows)
    branches = [
        functools.partial(team_program, n_rows, listed, shared, branch)
        for branch, (listed, shared) in enumerate((*TIERS, (size, size)))
    ]
    return lax.switch(tier[0], branches, code, lists, *args)


def either_device(*args):
    tiles, weights, labels = args[0], args[-1], args[5]
    n_rows, n_cols = lax.axis_size("rows"), lax.axis_size("cols")
    size, steps = tiles.shape[-1], tiles.shape[0]
    even = n_rows == 8 and steps * n_rows * 3 <= size and labels.shape[1] // n_cols % size == 0
    if even and size == 128 and weights.shape[1] == size * size:
        return team_device(*args)
    return per_device(*args)


def solution(mesh):
    return jax.shard_map(
        either_device,
        mesh=mesh,
        in_specs=(
            P(None, "rows", "cols", None, None, None),
            P(None, "rows", "cols", None),
            P(None, "rows", "cols", None),
            P(None, "rows", "cols", None),
            P(None, "rows", "cols"),
            P(None, "rows"),
            P(),
            P(None, ("cols", "rows")),
        ),
        out_specs=(P(None, ("cols", "rows")), P(None, ("rows", "cols"))),
        check_vma=False,
    )
```

```python
import functools
import math
import jax
import jax.numpy as jnp
from jax import lax
from jax.experimental import pallas as pl
from jax.experimental.pallas import tpu as pltpu
from jax.sharding import PartitionSpec as P

MESH = pl.DeviceIdType.MESH
VMEM_LIMIT = 48 * 1024 * 1024
VM = pl.BlockSpec(memory_space=pltpu.VMEM)
SM = pl.BlockSpec(memory_space=pltpu.SMEM)
LOCAL = pltpu.CompilerParams(vmem_limit_bytes=VMEM_LIMIT)
SLOTS = pltpu.CompilerParams(vmem_limit_bytes=48 * 1024 * 1024)


def lanes(block, size):
    return pl.ds(pl.multiple_of(block * size, size), size)


def pack_body(size, step, capacity, requests_ref, weights_ref, send_ref):
    owners = send_ref.shape[0] // capacity
    full = requests_ref.shape[1] // owners

    @pl.loop(0, capacity)
    def _(index):
        for peer in range(owners):
            where = lanes(requests_ref[step, peer * full + index], size)
            send_ref[peer * capacity + index] = weights_ref[:, where].astype(jnp.bfloat16)


def apply_body(size, step, capacity, requests_ref, rate_ref, weights_ref, grads_ref, out_ref):
    owners = grads_ref.shape[0] // capacity
    full = requests_ref.shape[1] // owners
    out_ref[...] = weights_ref[...]
    rate = rate_ref[step]

    @pl.loop(0, capacity)
    def _(index):
        for peer in range(owners):
            where = lanes(requests_ref[step, peer * full + index], size)
            grad = grads_ref[peer * capacity + index].astype(jnp.float32)
            out_ref[:, where] -= rate * grad


def apply_kernel(size, step, capacity, requests_ref, rate_ref, weights_ref, grads_ref, out_ref):
    apply_body(size, step, capacity, requests_ref, rate_ref, weights_ref, grads_ref, out_ref)


def apply_pack_kernel(
    size, step, capacity, requests_ref, rate_ref, weights_ref, grads_ref, out_ref, send_ref
):
    apply_body(size, step, capacity, requests_ref, rate_ref, weights_ref, grads_ref, out_ref)
    pack_body(size, step + 1, capacity, requests_ref, out_ref, send_ref)


def exchange_kernel(axis, count, send_ref, recv_ref, send_sems, recv_sems, own_sem):
    me = lax.axis_index(axis)
    barrier = pltpu.get_barrier_semaphore()
    for shift in range(1, count):
        peer = lax.rem(me + shift, count)
        pl.semaphore_signal(barrier, inc=1, device_id={axis: peer}, device_id_type=MESH)
    own = pltpu.make_async_copy(send_ref.at[me], recv_ref.at[me], own_sem)
    own.start()
    pl.semaphore_wait(barrier, count - 1)
    copies = []
    for shift in sorted(range(1, count), key=lambda shift: abs(2 * shift - count)):
        peer = lax.rem(me + shift, count)
        copy = pltpu.make_async_remote_copy(
            src_ref=send_ref.at[peer],
            dst_ref=recv_ref.at[me],
            send_sem=send_sems.at[shift],
            recv_sem=recv_sems.at[shift],
            device_id={axis: peer},
            device_id_type=MESH,
        )
        copy.start()
        copies.append(copy)
    own.wait()
    for copy in copies:
        copy.wait()


def exchange(send, axis, count, collective_id):
    return pl.pallas_call(
        functools.partial(exchange_kernel, axis, count),
        out_shape=jax.ShapeDtypeStruct(send.shape, send.dtype),
        in_specs=[VM],
        out_specs=VM,
        scratch_shapes=[
            pltpu.SemaphoreType.DMA((count,)),
            pltpu.SemaphoreType.DMA((count,)),
            pltpu.SemaphoreType.DMA,
        ],
        compiler_params=pltpu.CompilerParams(
            collective_id=collective_id, has_side_effects=True, vmem_limit_bytes=VMEM_LIMIT
        ),
        name="exchange",
    )(send)


def collect_kernel(n_rows, n_cols, mine_ref, all_ref, send_sems, recv_sems, own_sem):
    row, col = lax.axis_index("rows"), lax.axis_index("cols")
    row_peers = [lax.rem(row + shift, n_rows) for shift in range(1, n_rows)]
    col_peers = [lax.rem(col + shift, n_cols) for shift in range(1, n_cols)]
    barrier = pltpu.get_barrier_semaphore()
    for peer in row_peers:
        pl.semaphore_signal(barrier, inc=1, device_id={"rows": peer}, device_id_type=MESH)
    for peer in col_peers:
        pl.semaphore_signal(barrier, inc=1, device_id={"cols": peer}, device_id_type=MESH)
    own = pltpu.make_async_copy(mine_ref, all_ref.at[col, row], own_sem)
    own.start()
    pl.semaphore_wait(barrier, n_rows + n_cols - 2)
    copies = []
    for index, peer in enumerate(row_peers):
        copies.append(
            pltpu.make_async_remote_copy(
                src_ref=mine_ref,
                dst_ref=all_ref.at[col, row],
                send_sem=send_sems.at[index],
                recv_sem=recv_sems.at[index],
                device_id={"rows": peer},
                device_id_type=MESH,
            )
        )
        copies[-1].start()
    own.wait()
    for copy in copies:
        copy.wait()
    copies = []
    for index, peer in enumerate(col_peers):
        copies.append(
            pltpu.make_async_remote_copy(
                src_ref=all_ref.at[col],
                dst_ref=all_ref.at[col],
                send_sem=send_sems.at[n_rows + index],
                recv_sem=recv_sems.at[n_rows + index],
                device_id={"cols": peer},
                device_id_type=MESH,
            )
        )
        copies[-1].start()
    for copy in copies:
        copy.wait()


def collect(mine, n_rows, n_cols):
    return pl.pallas_call(
        functools.partial(collect_kernel, n_rows, n_cols),
        out_shape=jax.ShapeDtypeStruct((n_cols, n_rows, *mine.shape), mine.dtype),
        in_specs=[VM],
        out_specs=VM,
        scratch_shapes=[
            pltpu.SemaphoreType.DMA((n_rows + n_cols,)),
            pltpu.SemaphoreType.DMA((n_rows + n_cols,)),
            pltpu.SemaphoreType.DMA,
        ],
        compiler_params=pltpu.CompilerParams(collective_id=0, has_side_effects=True),
        name="collect",
    )(mine)


GROUP = 16


def slot_scalars(step, place_of, slot, code_ref, row_ref, scale_ref, count_ref):
    place = place_of(code_ref[step, slot])
    factor = jnp.where(slot < count_ref[step, 0, 0], scale_ref[step, 0, 0, slot], 0.0)
    return place, row_ref[step, 0, 0, slot], factor


def fetch_tiles(step, tiles_ref, held_ref, sems):
    def copy(group):
        part = pl.ds(group * GROUP, GROUP)
        return pltpu.make_async_copy(
            tiles_ref.at[step, 0, 0, part], held_ref.at[part], sems.at[group]
        )

    for group in range(held_ref.shape[0] // GROUP):
        copy(group).start()
    return lambda group: copy(group).wait()


def scores_kernel(
    step, place_of, code_ref, row_ref, scale_ref, count_ref, recv_ref, tiles_ref, out_ref,
    held_ref, sems,
):
    size = held_ref.shape[-1]
    arrived = fetch_tiles(step, tiles_ref, held_ref, sems)
    out_ref[...] = jnp.zeros_like(out_ref)

    @pl.loop(0, held_ref.shape[0] // GROUP)
    def _(group):
        arrived(group)
        products = []
        for lane in range(GROUP):
            slot = group * GROUP + lane
            place, row, factor = slot_scalars(
                step, place_of, slot, code_ref, row_ref, scale_ref, count_ref
            )
            product = lax.dot_general(
                recv_ref[place],
                held_ref[slot],
                (((1,), (1,)), ((), ())),
                preferred_element_type=jnp.float32,
            )
            products.append((row, product * factor))
        for row, product in products:
            out_ref[:, lanes(row, size)] += product


def classify_kernel(
    axis, count, step, part_ref, labels_ref, residual_ref, loss_ref, held, losses, send_sems,
    recv_sems,
):
    me = lax.axis_index(axis)
    barrier = pltpu.get_barrier_semaphore()
    for shift in range(1, count):
        peer = lax.rem(me + shift, count)
        pl.semaphore_signal(barrier, inc=1, device_id={axis: peer}, device_id_type=MESH)
    pl.semaphore_wait(barrier, count - 1)
    copies = []
    for shift in range(1, count):
        peer = lax.rem(me + shift, count)
        copy = pltpu.make_async_remote_copy(
            src_ref=part_ref,
            dst_ref=held.at[shift],
            send_sem=send_sems.at[shift],
            recv_sem=recv_sems.at[shift],
            device_id={axis: peer},
            device_id_type=MESH,
        )
        copy.start()
        copies.append(copy)
    scores = part_ref[...]
    for shift, copy in enumerate(copies):
        copy.wait()
        scores = scores + held[shift + 1]
    exp_scores = jnp.exp(scores)
    total = jnp.sum(exp_scores, axis=0, keepdims=True)
    class_ids = lax.broadcasted_iota(jnp.int32, scores.shape, 0)
    onehot = (class_ids == labels_ref[step : step + 1, :]).astype(jnp.float32)
    losses[...] = jnp.log(total) - jnp.sum(onehot * scores, axis=0, keepdims=True)
    if loss_ref.shape == losses.shape:
        loss_ref[...] = losses[...]
    else:
        loss_ref[...] = losses[:, lanes(me, loss_ref.shape[1])]
    residual_ref[...] = (exp_scores / total - onehot).astype(jnp.bfloat16)


def classify(step, n_cols, part, labels):
    classes, samples = part.shape
    owned = samples // n_cols
    return pl.pallas_call(
        functools.partial(classify_kernel, "cols", n_cols, step),
        out_shape=(
            jax.ShapeDtypeStruct((classes, samples), jnp.bfloat16),
            jax.ShapeDtypeStruct((1, owned if owned % 128 == 0 else samples), jnp.float32),
        ),
        in_specs=[VM, VM],
        out_specs=(VM, VM),
        scratch_shapes=[
            pltpu.VMEM((n_cols, classes, samples), jnp.float32),
            pltpu.VMEM((1, samples), jnp.float32),
            pltpu.SemaphoreType.DMA((n_cols,)),
            pltpu.SemaphoreType.DMA((n_cols,)),
        ],
        compiler_params=pltpu.CompilerParams(collective_id=1 + step, has_side_effects=True),
        name="classify",
    )(part, labels)


def grads_kernel(
    step, place_of, code_ref, row_ref, scale_ref, count_ref, residual_ref, tiles_ref,
    out_ref, total, held_ref, sems,
):
    size = held_ref.shape[-1]
    arrived = fetch_tiles(step, tiles_ref, held_ref, sems)
    total[...] = jnp.zeros_like(total)

    @pl.loop(0, held_ref.shape[0] // GROUP)
    def _(group):
        arrived(group)
        products = []
        for lane in range(GROUP):
            slot = group * GROUP + lane
            place, row, factor = slot_scalars(
                step, place_of, slot, code_ref, row_ref, scale_ref, count_ref
            )
            product = jnp.dot(
                residual_ref[:, lanes(row, size)],
                held_ref[slot],
                preferred_element_type=jnp.float32,
            )
            products.append((place, product * factor))
        for place, product in products:
            total[place] += product

    out_ref[...] = total[...].astype(jnp.bfloat16)


def sparse_program(
    capacity, branch, code, requests,
    tiles, tile_scales, tile_rows, tile_cols, tile_counts, labels, learning_rate, weights
):
    classes = weights.shape[0]
    size = tiles.shape[-1]
    steps = tiles.shape[0]
    n_rows, n_cols = lax.axis_size("rows"), lax.axis_size("cols")
    full = requests.shape[1] // n_rows
    samples = labels.shape[1]
    entries = n_rows * capacity
    packed = jax.ShapeDtypeStruct((entries, classes, size), jnp.bfloat16)
    owned = samples // n_cols
    scalars = (code, tile_rows, tile_scales, tile_counts)
    trade_id = 1 + steps + branch
    slots = tiles.shape[3]
    in_hbm = pl.BlockSpec(memory_space=pltpu.HBM)
    tile_room = [pltpu.VMEM(tiles.shape[3:], tiles.dtype), pltpu.SemaphoreType.DMA((slots // GROUP,))]

    def place_of(x):
        return x // full * capacity + lax.rem(x, full)

    def trade(x):
        blocks = x.reshape(n_rows, capacity, classes, size)
        return exchange(blocks, "rows", n_rows, trade_id).reshape(packed.shape)

    current = weights
    send = pl.pallas_call(
        functools.partial(pack_body, size, 0, capacity),
        out_shape=packed, in_specs=[SM, VM], out_specs=VM, compiler_params=LOCAL, name="pack",
    )(requests, current)
    losses = []
    for step in range(steps):
        got = trade(send)
        part = pl.pallas_call(
            functools.partial(scores_kernel, step, place_of),
            out_shape=jax.ShapeDtypeStruct((classes, samples), jnp.float32),
            in_specs=[SM] * 4 + [VM, in_hbm], out_specs=VM, compiler_params=SLOTS,
            scratch_shapes=tile_room, name="scores",
        )(*scalars, got, tiles)
        residual, loss = classify(step, n_cols, part, labels)
        if owned % 128 != 0:
            start = lax.axis_index("cols") * owned
            loss = lax.dynamic_slice_in_dim(loss, start, owned, axis=1)
        losses.append(loss)
        grads = pl.pallas_call(
            functools.partial(grads_kernel, step, place_of),
            out_shape=packed,
            in_specs=[SM] * 4 + [VM, in_hbm], out_specs=VM, compiler_params=SLOTS,
            scratch_shapes=[pltpu.VMEM((entries, classes, size), jnp.float32), *tile_room],
            name="grads",
        )(*scalars, residual, tiles)
        grads = trade(grads)
        shape = jax.ShapeDtypeStruct(current.shape, current.dtype)
        more = step + 1 < steps
        current, *send = pl.pallas_call(
            functools.partial(apply_pack_kernel if more else apply_kernel, size, step, capacity),
            out_shape=(shape, packed) if more else (shape,),
            in_specs=[SM, SM, VM, VM], out_specs=(VM, VM) if more else (VM,),
            compiler_params=LOCAL, name="apply",
        )(requests, learning_rate, current, grads)
        send = send[0] if more else None
    return current, jnp.concatenate(losses)


def per_device(
    tiles, tile_scales, tile_rows, tile_cols, tile_counts, labels, learning_rate, weights
):
    args = (tiles, tile_scales, tile_rows, tile_cols, tile_counts, labels, learning_rate, weights)
    size, slots = tiles.shape[-1], tiles.shape[3]
    n_rows, n_cols = lax.axis_size("rows"), lax.axis_size("cols")
    per_owner = weights.shape[1] // size
    full = min(per_owner, slots)
    mean = slots / n_rows
    tiers = [math.ceil(mean + spread * math.sqrt(mean)) for spread in (1.75, 2, 2.25, 2.5, 3, 4)]
    tiers = sorted({min(tier, full) for tier in tiers} | {full})
    slot_ids = jnp.arange(slots, dtype=jnp.int32)

    live = slot_ids < tile_counts[:, 0, 0, None]
    mine = jnp.where(live, tile_cols[:, 0, 0], -1)
    owner = jnp.where(live, mine // per_owner, -1)
    same = mine[:, :, None] == mine[:, None, :]
    before = slot_ids[:, None] > slot_ids[None, :]
    fresh = live & ~jnp.any(same & before, axis=-1)
    lower = (owner[:, :, None] == owner[:, None, :]) & (mine[:, None, :] < mine[:, :, None])
    rank = jnp.sum((lower & fresh[:, None, :]).astype(jnp.int32), axis=-1)
    code = jnp.where(live, owner * full + rank, 0)
    everyone = collect(jnp.where(fresh, mine * full + rank, -1), n_rows, n_cols)
    most = jnp.max(jnp.where(everyone >= 0, everyone % full, 0)) + 1

    row, col = lax.axis_index("rows"), lax.axis_index("cols")
    peers = lax.dynamic_index_in_dim(everyone, col, 0, keepdims=False)
    local = peers // full - row * per_owner
    asked = (peers >= 0) & (local >= 0) & (local < per_owner)
    order = jnp.where(asked, peers % full, -1)
    picks = order[..., None, :] == jnp.arange(full, dtype=jnp.int32)[:, None]
    wanted = jnp.sum(jnp.where(picks, local[..., None, :], 0), axis=-1)
    requests = jnp.swapaxes(wanted, 0, 1).reshape(-1, n_rows * full)

    def at_capacity(capacity, branch):
        return functools.partial(sparse_program, capacity, branch)

    branches = [at_capacity(capacity, branch) for branch, capacity in enumerate(tiers)]
    operands = (code, requests, *args)
    if len(branches) == 1:
        return branches[0](*operands)
    chosen = sum((most > tier).astype(jnp.int32) for tier in tiers[:-1])
    return lax.switch(chosen, branches, *operands)


SPILL = 12
TIERS = ((23, 14), (24, 16), (26, 18), (28, 22))
LEFT_RIGHT = (((1,), (1,)), ((), ()))


def teams(n_rows):
    team = n_rows // 2
    row = lax.axis_index("rows")
    half, place = row // team, lax.rem(row, team)
    mate = lambda shift: half * team + lax.rem(place + shift, team)
    other = lambda shift: (1 - half) * team + lax.rem(place + shift, team)
    return team, row, half, place, mate, other


def corners(place):
    beside = place + 1 - 2 * lax.rem(place, 2)
    return beside, lax.rem(place + 2, 4), lax.rem(beside + 2, 4)


def greet_rows(peers):
    barrier = pltpu.get_barrier_semaphore()
    for peer in peers:
        pl.semaphore_signal(barrier, inc=1, device_id={"rows": peer}, device_id_type=MESH)
    return lambda: pl.semaphore_wait(barrier, len(peers))


def slots_of(tile_cols, count, steps):
    slots = tile_cols.shape[1]
    ids = lax.broadcasted_iota(jnp.int32, (1, slots), 1)
    return [(tile_cols[s : s + 1, :], ids < count(s)) for s in range(steps)]


def mark_kernel(n_rows, n_cols, steps, cols_ref, count_ref, all_ref, mine, send_sems, recv_sems, own_sem):
    row, col = lax.axis_index("rows"), lax.axis_index("cols")
    row_peers = [lax.rem(row + shift, n_rows) for shift in range(1, n_rows)]
    col_peers = [lax.rem(col + shift, n_cols) for shift in range(1, n_cols)]
    barrier = pltpu.get_barrier_semaphore()
    for peer in row_peers:
        pl.semaphore_signal(barrier, inc=1, device_id={"rows": peer}, device_id_type=MESH)
    for peer in col_peers:
        pl.semaphore_signal(barrier, inc=1, device_id={"cols": peer}, device_id_type=MESH)
    size = mine.shape[1]
    marks = []
    for cols, live in slots_of(cols_ref[...], lambda s: count_ref[s, 0, 0], steps):
        slots = cols.shape[1]
        owners = lax.broadcasted_iota(jnp.int32, (n_rows, slots), 0)
        places = lax.broadcasted_iota(jnp.int32, (size, slots), 0)
        first = jnp.where(live & (cols >> 7 == owners), 1.0, 0.0).astype(jnp.bfloat16)
        second = jnp.where((cols & 127) == places, 1.0, 0.0).astype(jnp.bfloat16)
        count = lax.dot_general(first, second, LEFT_RIGHT, preferred_element_type=jnp.float32)
        marks.append(jnp.minimum(count, 1.0))
    mine[...] = jnp.concatenate(marks, axis=0).astype(jnp.bfloat16)
    pl.semaphore_wait(barrier, n_rows + n_cols - 2)
    own = pltpu.make_async_copy(mine, all_ref.at[col, row], own_sem)
    own.start()
    copies = []
    for index, peer in enumerate(row_peers):
        copies.append(
            pltpu.make_async_remote_copy(
                src_ref=mine,
                dst_ref=all_ref.at[col, row],
                send_sem=send_sems.at[index],
                recv_sem=recv_sems.at[index],
                device_id={"rows": peer},
                device_id_type=MESH,
            )
        )
        copies[-1].start()
    own.wait()
    for copy in copies:
        copy.wait()
    copies = []
    for index, peer in enumerate(col_peers):
        copies.append(
            pltpu.make_async_remote_copy(
                src_ref=all_ref.at[col],
                dst_ref=all_ref.at[col],
                send_sem=send_sems.at[n_rows + index],
                recv_sem=recv_sems.at[n_rows + index],
                device_id={"cols": peer},
                device_id_type=MESH,
            )
        )
        copies[-1].start()
    for copy in copies:
        copy.wait()


def mark(tile_cols, tile_counts, n_rows, n_cols, size):
    steps = tile_cols.shape[0]
    return pl.pallas_call(
        functools.partial(mark_kernel, n_rows, n_cols, steps),
        out_shape=jax.ShapeDtypeStruct((n_cols, n_rows, steps * n_rows, size), jnp.bfloat16),
        in_specs=[VM, SM],
        out_specs=VM,
        scratch_shapes=[
            pltpu.VMEM((steps * n_rows, size), jnp.bfloat16),
            pltpu.SemaphoreType.DMA((n_rows + n_cols,)),
            pltpu.SemaphoreType.DMA((n_rows + n_cols,)),
            pltpu.SemaphoreType.DMA,
        ],
        compiler_params=pltpu.CompilerParams(collective_id=0, has_side_effects=True),
        name="mark",
    )(tile_cols, tile_counts)


def plan_kernel(
    n_rows, steps, all_ref, cols_ref, count_ref, code_ref, list_ref, tier_ref, keys, shared_keys, table
):
    team, row, half, _, _, _ = teams(n_rows)
    col = lax.axis_index("cols")
    size = all_ref.shape[-1]
    n_cols = all_ref.shape[0]
    depth = steps * n_rows
    before = lax.broadcasted_iota(jnp.int32, (size, size), 0)
    after = lax.broadcasted_iota(jnp.int32, (size, size), 1)
    triangle = jnp.where(before < after, 1.0, 0.0).astype(jnp.bfloat16)

    def ranks(flags):
        flat = flags.reshape(-1, size).astype(jnp.bfloat16)
        return jnp.dot(flat, triangle, preferred_element_type=jnp.float32).reshape(flags.shape)

    owner = lax.rem(lax.broadcasted_iota(jnp.int32, (1, depth, size), 1), n_rows)
    most_listed, most_shared = [], []
    for part in range(2):
        needs = all_ref[:, part * team : (part + 1) * team].astype(jnp.float32)
        near = owner // team == part
        wanted = needs[:, 0]
        for index in range(1, team):
            wanted = wanted + needs[:, index]
        alone = near | (wanted < 1.5)
        listed = jnp.where(alone[:, None], needs, 0.0)
        rank = ranks(listed)
        over = jnp.where(rank >= SPILL, listed, 0.0)
        spilled = over[:, 0]
        for index in range(1, team):
            spilled = jnp.maximum(spilled, over[:, index])
        shared = jnp.where(near | ((wanted < 1.5) & (spilled < 0.5)), 0.0, 1.0)
        shared_rank = ranks(shared)
        keep = (listed > 0.5) & (near[:, None] | (rank < SPILL))
        keys[:, part * team : (part + 1) * team] = jnp.where(keep, rank, -1.0)
        shared_keys[:, part] = jnp.where(shared > 0.5, shared_rank, -1.0)
        most_listed.append(jnp.max(jnp.where(keep & near[:, None], rank, -1.0)))
        most_shared.append(jnp.max(jnp.where(shared > 0.5, shared_rank, -1.0)))
    listed = jnp.maximum(*most_listed) + 1.0
    shared = jnp.maximum(*most_shared) + 1.0
    tier = jnp.int32(0)
    for cap, shared_cap in TIERS:
        tier = tier + jnp.where((listed > cap) | (shared > shared_cap), 1, 0).astype(jnp.int32)
    tier_ref[0] = tier

    table[...] = jnp.full_like(table, -1.0)
    sub = lax.broadcasted_iota(jnp.int32, (n_rows, size), 0)
    slot = lax.rem(sub, team)
    n_lists = 2 * team + 1
    for s in range(steps):
        mine = pl.ds(s * n_rows + row, 1)
        for index in range(team):
            at = 2 * n_rows * s + index
            table[at : at + 1, :] = keys[col, half * team + index, mine, :]
            table[at + team : at + team + 1, :] = keys[col, (1 - half) * team + index, mine, :]
        at = 2 * n_rows * s + 2 * team
        table[at : at + 1, :] = shared_keys[col, 1 - half, mine, :]
        block = pl.ds(s * n_rows, n_rows)
        listed_key = keys[col, row, block, :]
        shared_key = shared_keys[col, half, block, :]
        kind = jnp.where(sub // team == half, slot, team + slot)
        value = (kind * size).astype(jnp.float32) + listed_key
        other = ((2 * team + slot) * size).astype(jnp.float32) + shared_key
        at = 2 * n_rows * steps + s * n_rows
        table[at : at + n_rows, :] = jnp.where(shared_key >= 0.0, other, value)
    flipped = table[...].T
    lane = after.astype(jnp.float32)
    down = before.astype(jnp.float32)
    for s in range(steps):
        for index in range(n_lists):
            at = 2 * n_rows * s + index
            hit = flipped[:, at : at + 1] == lane
            picked = jnp.sum(jnp.where(hit, down, 0.0), axis=0, keepdims=True)
            list_ref[s : s + 1, index * size : (index + 1) * size] = picked.astype(jnp.int32)
    for s, (cols, live) in enumerate(slots_of(cols_ref[...], lambda s: count_ref[s, 0, 0], steps)):
        chosen = jnp.zeros((size, size), jnp.float32)
        for index in range(n_rows):
            at = 2 * n_rows * steps + s * n_rows + index
            chosen = jnp.where(cols >> 7 == index, flipped[:, at : at + 1], chosen)
        code = jnp.sum(jnp.where((cols & 127) == before, chosen, 0.0), axis=0, keepdims=True)
        code_ref[s : s + 1, :] = jnp.where(live, code, 0.0).astype(jnp.int32)


def plan(everyone, tile_cols, tile_counts, n_rows):
    steps, slots = tile_cols.shape
    size = everyone.shape[-1]
    lists = n_rows + 1
    return pl.pallas_call(
        functools.partial(plan_kernel, n_rows, steps),
        out_shape=(
            jax.ShapeDtypeStruct((steps, slots), jnp.int32),
            jax.ShapeDtypeStruct((steps, lists * size), jnp.int32),
            jax.ShapeDtypeStruct((1,), jnp.int32),
        ),
        in_specs=[VM, VM, SM],
        out_specs=(VM, VM, SM),
        scratch_shapes=[
            pltpu.VMEM(everyone.shape, jnp.float32),
            pltpu.VMEM((everyone.shape[0], 2, *everyone.shape[2:]), jnp.float32),
            pltpu.VMEM((size, size), jnp.float32),
        ],
        compiler_params=LOCAL,
        name="plan",
    )(everyone, tile_cols, tile_counts)


def split_classify_kernel(
    count, step, part_ref, labels_ref, residual_ref, loss_ref, held, send_sems, recv_sems
):
    me = lax.axis_index("cols")
    owned = loss_ref.shape[1]
    barrier = pltpu.get_barrier_semaphore()
    peers = [lax.rem(me + shift, count) for shift in range(1, count)]
    for peer in peers:
        pl.semaphore_signal(barrier, inc=1, device_id={"cols": peer}, device_id_type=MESH)
    mine = lanes(me, owned)

    def copy(index, src, dst, peer):
        return pltpu.make_async_remote_copy(
            src_ref=src,
            dst_ref=dst,
            send_sem=send_sems.at[index],
            recv_sem=recv_sems.at[index],
            device_id={"cols": peer},
            device_id_type=MESH,
        )

    pl.semaphore_wait(barrier, count - 1)
    parts = [copy(i, part_ref.at[:, lanes(peer, owned)], held.at[i], peer) for i, peer in enumerate(peers)]
    for part in parts:
        part.start()
    class_ids = lax.broadcasted_iota(jnp.int32, held.shape[1:], 0)
    onehot = (class_ids == labels_ref[step : step + 1, mine]).astype(jnp.float32)
    scores = part_ref[:, mine]
    for index, part in enumerate(parts):
        part.wait_recv()
        scores = scores + held[index]
    exp_scores = jnp.exp(scores)
    total = jnp.sum(exp_scores, axis=0, keepdims=True)
    residual_ref[:, mine] = (exp_scores / total - onehot).astype(jnp.bfloat16)
    loss_ref[...] = jnp.log(total) - jnp.sum(onehot * scores, axis=0, keepdims=True)
    shared = residual_ref.at[:, mine]
    sent = [copy(count + i, shared, shared, peer) for i, peer in enumerate(peers)]
    for part in sent:
        part.start()
    for part in parts:
        part.wait_send()
    for part in sent:
        part.wait()


def split_classify(step, n_cols, part, labels):
    classes, samples = part.shape
    owned = samples // n_cols
    return pl.pallas_call(
        functools.partial(split_classify_kernel, n_cols, step),
        out_shape=(
            jax.ShapeDtypeStruct((classes, samples), jnp.bfloat16),
            jax.ShapeDtypeStruct((1, owned), jnp.float32),
        ),
        in_specs=[VM, VM],
        out_specs=(VM, VM),
        scratch_shapes=[
            pltpu.VMEM((n_cols - 1, classes, owned), jnp.float32),
            pltpu.SemaphoreType.DMA((2 * n_cols,)),
            pltpu.SemaphoreType.DMA((2 * n_cols,)),
        ],
        compiler_params=pltpu.CompilerParams(
            collective_id=1 + step, has_side_effects=True, vmem_limit_bytes=VMEM_LIMIT
        ),
        name="classify",
    )(part, labels)


class Room:
    def __init__(self, team, listed, shared):
        self.team, self.listed, self.shared = team, listed, shared
        self.spill = team * listed
        self.common = self.spill + team * SPILL
        self.packed = self.common + shared
        self.spread = self.common + team * shared

    def near(self, index):
        return pl.ds(index * self.listed, self.listed)

    def far(self, index):
        return pl.ds(self.spill + index * SPILL, SPILL)

    def group(self, index):
        return pl.ds(self.common + index * self.shared, self.shared)

    def place(self, code, size):
        kind, rank = code // size, lax.rem(code, size)
        far = self.spill + (kind - self.team) * SPILL
        common = self.common + (kind - 2 * self.team) * self.shared
        base = jnp.where(kind < 2 * self.team, far, common)
        return jnp.where(kind < self.team, kind * self.listed, base) + rank

    def entries(self, body):
        def run(first, lists, count, start):
            @pl.loop(0, count)
            def _(index):
                for which in range(lists):
                    body(start + which * count + index, first + which, index)

        run(0, self.team, self.listed, 0)
        run(self.team, self.team, SPILL, self.spill)
        run(2 * self.team, 1, self.shared, self.common)


def pack_lists(room, step, lists_ref, weights_ref, send_ref):
    size = send_ref.shape[-1]

    def body(entry, which, index):
        where = lanes(lists_ref[step, which * size + index], size)
        send_ref[entry] = weights_ref[:, where].astype(jnp.bfloat16)

    room.entries(body)


def apply_lists(room, step, lists_ref, rate_ref, weights_ref, grads_ref, out_ref):
    size = grads_ref.shape[-1]
    out_ref[...] = weights_ref[...]
    rate = rate_ref[step]

    def body(entry, which, index):
        where = lanes(lists_ref[step, which * size + index], size)
        out_ref[:, where] -= rate * grads_ref[entry].astype(jnp.float32)

    room.entries(body)


def apply_pack_lists(room, step, lists_ref, rate_ref, weights_ref, grads_ref, out_ref, send_ref):
    apply_lists(room, step, lists_ref, rate_ref, weights_ref, grads_ref, out_ref)
    pack_lists(room, step + 1, lists_ref, out_ref, send_ref)


def row_copy(sems, index, src, dst, peer):
    return pltpu.make_async_remote_copy(
        src_ref=src,
        dst_ref=dst,
        send_sem=sems[0].at[index],
        recv_sem=sems[1].at[index],
        device_id={"rows": peer},
        device_id_type=MESH,
    )


def spread_kernel(room, n_rows, send, got_ref, send_sems, recv_sems, own_sem):
    team, _, half, place, _, other = teams(n_rows)
    sems = (send_sems, recv_sems)
    beside, across, corner = corners(place)
    entered = greet_rows([half * team + to for to in (beside, across, corner)] + [other(s) for s in range(team)])

    def to_mate(index, src, dst, mate):
        copies.append(row_copy(sems, index, src, got_ref.at[dst], half * team + mate))
        copies[-1].start()
        return copies[-1]

    copies = []
    common = pl.ds(room.common, room.shared)
    own = pltpu.make_async_copy(send.at[room.near(place)], got_ref.at[room.near(place)], own_sem)
    own.start()
    entered()
    group = row_copy(sems, 0, send.at[common], got_ref.at[room.group(place)], other(0))
    group.start()
    for shift in range(team):
        to = lax.rem(place + shift, team)
        copies.append(row_copy(
            sems, 1 + shift, send.at[room.far(to)], got_ref.at[room.far(place)], other(shift)
        ))
        copies[-1].start()
    to_mate(8, send.at[room.near(beside)], room.near(place), beside)
    group.wait_recv()
    mine = room.group(place)
    passed = to_mate(6, got_ref.at[mine], mine, across)
    to_mate(5, got_ref.at[mine], mine, beside)
    to_mate(9, send.at[room.near(across)], room.near(place), across)
    to_mate(10, send.at[room.near(corner)], room.near(place), corner)

    passed.wait_recv()
    theirs = room.group(across)
    to_mate(7, got_ref.at[theirs], theirs, beside)
    passed.wait_send()
    group.wait_send()
    own.wait()
    for copy in copies:
        if copy is not passed:
            copy.wait()


def gather_kernel(
    room, n_rows, grads_ref, out_ref, pool, passing, total, send_sems, recv_sems, own_sem
):
    team, _, half, place, _, other = teams(n_rows)
    sems = (send_sems, recv_sems)
    beside, across, corner = corners(place)
    entered = greet_rows([half * team + to for to in (beside, across, corner)] + [other(s) for s in range(team)])
    own = pltpu.make_async_copy(grads_ref.at[room.near(place)], out_ref.at[room.near(place)], own_sem)
    own.start()
    entered()

    def to_mate(index, src, dst, mate):
        copy = row_copy(sems, index, src, dst, half * team + mate)
        copy.start()
        return copy

    def near(index, to):
        copies.append(to_mate(index, grads_ref.at[room.near(to)], out_ref.at[room.near(place)], to))

    copies = []
    onward = to_mate(6, grads_ref.at[room.group(corner)], pool.at[0], beside)
    direct = to_mate(5, grads_ref.at[room.group(beside)], pool.at[1], beside)
    for shift in range(team):
        to = lax.rem(place + shift, team)
        copies.append(row_copy(
            sems, 1 + shift, grads_ref.at[room.far(to)], out_ref.at[room.far(place)], other(shift)
        ))
        copies[-1].start()
    near(8, beside)
    onward.wait_recv()

    def add(first, parts, into):
        @pl.loop(0, room.shared)
        def _(index):
            value = grads_ref[first + index].astype(jnp.float32)
            for part in parts:
                value = value + pool[part, index].astype(jnp.float32)
            into[index] = value.astype(jnp.bfloat16)

    add(room.common + across * room.shared, (0,), passing)
    passed = to_mate(7, passing, pool.at[2], across)
    near(9, across)
    direct.wait_recv()
    passed.wait_recv()
    add(room.common + place * room.shared, (1, 2), total)
    common = pl.ds(room.common, room.shared)
    group = row_copy(sems, 0, total, out_ref.at[common], other(0))
    group.start()
    near(10, corner)
    for copy in (onward, direct, passed):
        copy.wait_send()
    own.wait()
    for copy in copies:
        copy.wait()
    group.wait()


def remote_sems(count):
    return [pltpu.SemaphoreType.DMA((count,)), pltpu.SemaphoreType.DMA((count,)), pltpu.SemaphoreType.DMA]


def team_program(
    n_rows, listed, shared, branch, code, lists,
    tiles, tile_scales, tile_rows, tile_cols, tile_counts, labels, learning_rate, weights
):
    classes = weights.shape[0]
    size = tiles.shape[-1]
    steps, slots = tiles.shape[0], tiles.shape[3]
    n_cols = lax.axis_size("cols")
    samples = labels.shape[1]
    owned = samples // n_cols
    room = Room(n_rows // 2, listed, shared)
    packed = jax.ShapeDtypeStruct((room.packed, classes, size), jnp.bfloat16)
    spread = jax.ShapeDtypeStruct((room.spread, classes, size), jnp.bfloat16)
    scalars = (code, tile_rows, tile_scales, tile_counts)
    in_hbm = pl.BlockSpec(memory_space=pltpu.HBM)
    tile_room = [pltpu.VMEM(tiles.shape[3:], tiles.dtype), pltpu.SemaphoreType.DMA((slots // GROUP,))]

    def remote(index):
        return pltpu.CompilerParams(
            collective_id=1 + steps + 2 * branch + index, has_side_effects=True,
            vmem_limit_bytes=VMEM_LIMIT,
        )

    current = weights
    send = pl.pallas_call(
        functools.partial(pack_lists, room, 0),
        out_shape=packed, in_specs=[SM, VM], out_specs=VM, compiler_params=LOCAL, name="pack",
    )(lists, current)
    losses = []
    for step in range(steps):
        got = pl.pallas_call(
            functools.partial(spread_kernel, room, n_rows),
            out_shape=spread, in_specs=[VM], out_specs=VM, compiler_params=remote(0),
            scratch_shapes=remote_sems(11), name="spread",
        )(send)
        part = pl.pallas_call(
            functools.partial(scores_kernel, step, lambda x: room.place(x, size)),
            out_shape=jax.ShapeDtypeStruct((classes, samples), jnp.float32),
            in_specs=[SM] * 4 + [VM, in_hbm], out_specs=VM, compiler_params=SLOTS,
            scratch_shapes=tile_room, name="scores",
        )(*scalars, got, tiles)
        residual, loss = split_classify(step, n_cols, part, labels)
        losses.append(loss)
        grads = pl.pallas_call(
            functools.partial(grads_kernel, step, lambda x: room.place(x, size)),
            out_shape=spread,
            in_specs=[SM] * 4 + [VM, in_hbm], out_specs=VM, compiler_params=SLOTS,
            scratch_shapes=[pltpu.VMEM((room.spread, classes, size), jnp.float32), *tile_room],
            name="grads",
        )(*scalars, residual, tiles)
        grads = pl.pallas_call(
            functools.partial(gather_kernel, room, n_rows),
            out_shape=packed, in_specs=[VM], out_specs=VM, compiler_params=remote(1),
            scratch_shapes=[
                pltpu.VMEM((3, shared, classes, size), jnp.bfloat16),
                pltpu.VMEM((shared, classes, size), jnp.bfloat16),
                pltpu.VMEM((shared, classes, size), jnp.bfloat16),
                *remote_sems(11),
            ],
            name="gather",
        )(grads)
        shape = jax.ShapeDtypeStruct(current.shape, current.dtype)
        more = step + 1 < steps
        current, *send = pl.pallas_call(
            functools.partial(apply_pack_lists if more else apply_lists, room, step),
            out_shape=(shape, packed) if more else (shape,),
            in_specs=[SM, SM, VM, VM], out_specs=(VM, VM) if more else (VM,),
            compiler_params=LOCAL, name="apply",
        )(lists, learning_rate, current, grads)
        send = send[0] if more else None
    return current, jnp.concatenate(losses)


def team_device(
    tiles, tile_scales, tile_rows, tile_cols, tile_counts, labels, learning_rate, weights
):
    args = (tiles, tile_scales, tile_rows, tile_cols, tile_counts, labels, learning_rate, weights)
    size = tiles.shape[-1]
    n_rows, n_cols = lax.axis_size("rows"), lax.axis_size("cols")
    cols = tile_cols[:, 0, 0]
    everyone = mark(cols, tile_counts, n_rows, n_cols, size)
    code, lists, tier = plan(everyone, cols, tile_counts, n_rows)
    branches = [
        functools.partial(team_program, n_rows, listed, shared, branch)
        for branch, (listed, shared) in enumerate((*TIERS, (size, size)))
    ]
    return lax.switch(tier[0], branches, code, lists, *args)


def either_device(*args):
    tiles, weights, labels = args[0], args[-1], args[5]
    n_rows, n_cols = lax.axis_size("rows"), lax.axis_size("cols")
    size, steps = tiles.shape[-1], tiles.shape[0]
    even = n_rows == 8 and steps * n_rows * 3 <= size and labels.shape[1] // n_cols % size == 0
    if even and size == 128 and weights.shape[1] == size * size:
        return team_device(*args)
    return per_device(*args)


def solution(mesh):
    return jax.shard_map(
        either_device,
        mesh=mesh,
        in_specs=(
            P(None, "rows", "cols", None, None, None),
            P(None, "rows", "cols", None),
            P(None, "rows", "cols", None),
            P(None, "rows", "cols", None),
            P(None, "rows", "cols"),
            P(None, "rows"),
            P(),
            P(None, ("cols", "rows")),
        ),
        out_specs=(P(None, ("cols", "rows")), P(None, ("rows", "cols"))),
        check_vma=False,
    )
```

```python
import functools
import math
import jax
import jax.numpy as jnp
from jax import lax
from jax.experimental import pallas as pl
from jax.experimental.pallas import tpu as pltpu
from jax.sharding import PartitionSpec as P

MESH = pl.DeviceIdType.MESH
VMEM_LIMIT = 48 * 1024 * 1024
VM = pl.BlockSpec(memory_space=pltpu.VMEM)
SM = pl.BlockSpec(memory_space=pltpu.SMEM)
LOCAL = pltpu.CompilerParams(vmem_limit_bytes=VMEM_LIMIT)
SLOTS = pltpu.CompilerParams(vmem_limit_bytes=48 * 1024 * 1024)


def lanes(block, size):
    return pl.ds(pl.multiple_of(block * size, size), size)


def pack_body(size, step, capacity, requests_ref, weights_ref, send_ref):
    owners = send_ref.shape[0] // capacity
    full = requests_ref.shape[1] // owners

    @pl.loop(0, capacity)
    def _(index):
        for peer in range(owners):
            where = lanes(requests_ref[step, peer * full + index], size)
            send_ref[peer * capacity + index] = weights_ref[:, where].astype(jnp.bfloat16)


def apply_body(size, step, capacity, requests_ref, rate_ref, weights_ref, grads_ref, out_ref):
    owners = grads_ref.shape[0] // capacity
    full = requests_ref.shape[1] // owners
    out_ref[...] = weights_ref[...]
    rate = rate_ref[step]

    @pl.loop(0, capacity)
    def _(index):
        for peer in range(owners):
            where = lanes(requests_ref[step, peer * full + index], size)
            grad = grads_ref[peer * capacity + index].astype(jnp.float32)
            out_ref[:, where] -= rate * grad


def apply_kernel(size, step, capacity, requests_ref, rate_ref, weights_ref, grads_ref, out_ref):
    apply_body(size, step, capacity, requests_ref, rate_ref, weights_ref, grads_ref, out_ref)


def apply_pack_kernel(
    size, step, capacity, requests_ref, rate_ref, weights_ref, grads_ref, out_ref, send_ref
):
    apply_body(size, step, capacity, requests_ref, rate_ref, weights_ref, grads_ref, out_ref)
    pack_body(size, step + 1, capacity, requests_ref, out_ref, send_ref)


def exchange_kernel(axis, count, send_ref, recv_ref, send_sems, recv_sems, own_sem):
    me = lax.axis_index(axis)
    barrier = pltpu.get_barrier_semaphore()
    for shift in range(1, count):
        peer = lax.rem(me + shift, count)
        pl.semaphore_signal(barrier, inc=1, device_id={axis: peer}, device_id_type=MESH)
    own = pltpu.make_async_copy(send_ref.at[me], recv_ref.at[me], own_sem)
    own.start()
    pl.semaphore_wait(barrier, count - 1)
    copies = []
    for shift in sorted(range(1, count), key=lambda shift: abs(2 * shift - count)):
        peer = lax.rem(me + shift, count)
        copy = pltpu.make_async_remote_copy(
            src_ref=send_ref.at[peer],
            dst_ref=recv_ref.at[me],
            send_sem=send_sems.at[shift],
            recv_sem=recv_sems.at[shift],
            device_id={axis: peer},
            device_id_type=MESH,
        )
        copy.start()
        copies.append(copy)
    own.wait()
    for copy in copies:
        copy.wait()


def exchange(send, axis, count, collective_id):
    return pl.pallas_call(
        functools.partial(exchange_kernel, axis, count),
        out_shape=jax.ShapeDtypeStruct(send.shape, send.dtype),
        in_specs=[VM],
        out_specs=VM,
        scratch_shapes=[
            pltpu.SemaphoreType.DMA((count,)),
            pltpu.SemaphoreType.DMA((count,)),
            pltpu.SemaphoreType.DMA,
        ],
        compiler_params=pltpu.CompilerParams(
            collective_id=collective_id, has_side_effects=True, vmem_limit_bytes=VMEM_LIMIT
        ),
        name="exchange",
    )(send)


def collect_kernel(n_rows, n_cols, mine_ref, all_ref, send_sems, recv_sems, own_sem):
    row, col = lax.axis_index("rows"), lax.axis_index("cols")
    row_peers = [lax.rem(row + shift, n_rows) for shift in range(1, n_rows)]
    col_peers = [lax.rem(col + shift, n_cols) for shift in range(1, n_cols)]
    barrier = pltpu.get_barrier_semaphore()
    for peer in row_peers:
        pl.semaphore_signal(barrier, inc=1, device_id={"rows": peer}, device_id_type=MESH)
    for peer in col_peers:
        pl.semaphore_signal(barrier, inc=1, device_id={"cols": peer}, device_id_type=MESH)
    own = pltpu.make_async_copy(mine_ref, all_ref.at[col, row], own_sem)
    own.start()
    pl.semaphore_wait(barrier, n_rows + n_cols - 2)
    copies = []
    for index, peer in enumerate(row_peers):
        copies.append(
            pltpu.make_async_remote_copy(
                src_ref=mine_ref,
                dst_ref=all_ref.at[col, row],
                send_sem=send_sems.at[index],
                recv_sem=recv_sems.at[index],
                device_id={"rows": peer},
                device_id_type=MESH,
            )
        )
        copies[-1].start()
    own.wait()
    for copy in copies:
        copy.wait()
    copies = []
    for index, peer in enumerate(col_peers):
        copies.append(
            pltpu.make_async_remote_copy(
                src_ref=all_ref.at[col],
                dst_ref=all_ref.at[col],
                send_sem=send_sems.at[n_rows + index],
                recv_sem=recv_sems.at[n_rows + index],
                device_id={"cols": peer},
                device_id_type=MESH,
            )
        )
        copies[-1].start()
    for copy in copies:
        copy.wait()


def collect(mine, n_rows, n_cols):
    return pl.pallas_call(
        functools.partial(collect_kernel, n_rows, n_cols),
        out_shape=jax.ShapeDtypeStruct((n_cols, n_rows, *mine.shape), mine.dtype),
        in_specs=[VM],
        out_specs=VM,
        scratch_shapes=[
            pltpu.SemaphoreType.DMA((n_rows + n_cols,)),
            pltpu.SemaphoreType.DMA((n_rows + n_cols,)),
            pltpu.SemaphoreType.DMA,
        ],
        compiler_params=pltpu.CompilerParams(collective_id=0, has_side_effects=True),
        name="collect",
    )(mine)


GROUP = 16


def slot_scalars(step, place_of, slot, code_ref, row_ref, scale_ref, count_ref):
    place = place_of(code_ref[step, slot])
    count = count_ref[(step,) + (0,) * (len(count_ref.shape) - 1)]
    factor = jnp.where(slot < count, scale_ref[step, 0, 0, slot], 0.0)
    return place, row_ref[step, 0, 0, slot], factor


def fetch_tiles(step, tiles_ref, held_ref, sems):
    def copy(group):
        part = pl.ds(group * GROUP, GROUP)
        return pltpu.make_async_copy(
            tiles_ref.at[step, 0, 0, part], held_ref.at[part], sems.at[group]
        )

    for group in range(held_ref.shape[0] // GROUP):
        copy(group).start()
    return lambda group: copy(group).wait()


def scores_kernel(
    step, place_of, code_ref, row_ref, scale_ref, count_ref, recv_ref, tiles_ref, out_ref,
    held_ref, sems,
):
    size = held_ref.shape[-1]
    arrived = fetch_tiles(step, tiles_ref, held_ref, sems)
    out_ref[...] = jnp.zeros_like(out_ref)

    @pl.loop(0, held_ref.shape[0] // GROUP)
    def _(group):
        arrived(group)
        products = []
        for lane in range(GROUP):
            slot = group * GROUP + lane
            place, row, factor = slot_scalars(
                step, place_of, slot, code_ref, row_ref, scale_ref, count_ref
            )
            product = lax.dot_general(
                recv_ref[place],
                held_ref[slot],
                (((1,), (1,)), ((), ())),
                preferred_element_type=jnp.float32,
            )
            products.append((row, product * factor))
        for row, product in products:
            out_ref[:, lanes(row, size)] += product


def classify_kernel(
    axis, count, step, part_ref, labels_ref, residual_ref, loss_ref, held, losses, send_sems,
    recv_sems,
):
    me = lax.axis_index(axis)
    barrier = pltpu.get_barrier_semaphore()
    for shift in range(1, count):
        peer = lax.rem(me + shift, count)
        pl.semaphore_signal(barrier, inc=1, device_id={axis: peer}, device_id_type=MESH)
    pl.semaphore_wait(barrier, count - 1)
    copies = []
    for shift in range(1, count):
        peer = lax.rem(me + shift, count)
        copy = pltpu.make_async_remote_copy(
            src_ref=part_ref,
            dst_ref=held.at[shift],
            send_sem=send_sems.at[shift],
            recv_sem=recv_sems.at[shift],
            device_id={axis: peer},
            device_id_type=MESH,
        )
        copy.start()
        copies.append(copy)
    scores = part_ref[...]
    for shift, copy in enumerate(copies):
        copy.wait()
        scores = scores + held[shift + 1]
    exp_scores = jnp.exp(scores)
    total = jnp.sum(exp_scores, axis=0, keepdims=True)
    class_ids = lax.broadcasted_iota(jnp.int32, scores.shape, 0)
    onehot = (class_ids == labels_ref[step : step + 1, :]).astype(jnp.float32)
    losses[...] = jnp.log(total) - jnp.sum(onehot * scores, axis=0, keepdims=True)
    if loss_ref.shape == losses.shape:
        loss_ref[...] = losses[...]
    else:
        loss_ref[...] = losses[:, lanes(me, loss_ref.shape[1])]
    residual_ref[...] = (exp_scores / total - onehot).astype(jnp.bfloat16)


def classify(step, n_cols, part, labels):
    classes, samples = part.shape
    owned = samples // n_cols
    return pl.pallas_call(
        functools.partial(classify_kernel, "cols", n_cols, step),
        out_shape=(
            jax.ShapeDtypeStruct((classes, samples), jnp.bfloat16),
            jax.ShapeDtypeStruct((1, owned if owned % 128 == 0 else samples), jnp.float32),
        ),
        in_specs=[VM, VM],
        out_specs=(VM, VM),
        scratch_shapes=[
            pltpu.VMEM((n_cols, classes, samples), jnp.float32),
            pltpu.VMEM((1, samples), jnp.float32),
            pltpu.SemaphoreType.DMA((n_cols,)),
            pltpu.SemaphoreType.DMA((n_cols,)),
        ],
        compiler_params=pltpu.CompilerParams(collective_id=1 + step, has_side_effects=True),
        name="classify",
    )(part, labels)


def grads_kernel(
    step, place_of, code_ref, row_ref, scale_ref, count_ref, residual_ref, tiles_ref,
    out_ref, total, held_ref, sems,
):
    size = held_ref.shape[-1]
    arrived = fetch_tiles(step, tiles_ref, held_ref, sems)
    total[...] = jnp.zeros_like(total)

    @pl.loop(0, held_ref.shape[0] // GROUP)
    def _(group):
        arrived(group)
        products = []
        for lane in range(GROUP):
            slot = group * GROUP + lane
            place, row, factor = slot_scalars(
                step, place_of, slot, code_ref, row_ref, scale_ref, count_ref
            )
            product = jnp.dot(
                residual_ref[:, lanes(row, size)],
                held_ref[slot],
                preferred_element_type=jnp.float32,
            )
            products.append((place, product * factor))
        for place, product in products:
            total[place] += product

    out_ref[...] = total[...].astype(jnp.bfloat16)


def sparse_program(
    capacity, branch, code, requests,
    tiles, tile_scales, tile_rows, tile_cols, tile_counts, labels, learning_rate, weights
):
    classes = weights.shape[0]
    size = tiles.shape[-1]
    steps = tiles.shape[0]
    n_rows, n_cols = lax.axis_size("rows"), lax.axis_size("cols")
    full = requests.shape[1] // n_rows
    samples = labels.shape[1]
    entries = n_rows * capacity
    packed = jax.ShapeDtypeStruct((entries, classes, size), jnp.bfloat16)
    owned = samples // n_cols
    scalars = (code, tile_rows, tile_scales, tile_counts)
    trade_id = 1 + steps + branch
    slots = tiles.shape[3]
    in_hbm = pl.BlockSpec(memory_space=pltpu.HBM)
    tile_room = [pltpu.VMEM(tiles.shape[3:], tiles.dtype), pltpu.SemaphoreType.DMA((slots // GROUP,))]

    def place_of(x):
        return x // full * capacity + lax.rem(x, full)

    def trade(x):
        blocks = x.reshape(n_rows, capacity, classes, size)
        return exchange(blocks, "rows", n_rows, trade_id).reshape(packed.shape)

    current = weights
    send = pl.pallas_call(
        functools.partial(pack_body, size, 0, capacity),
        out_shape=packed, in_specs=[SM, VM], out_specs=VM, compiler_params=LOCAL, name="pack",
    )(requests, current)
    losses = []
    for step in range(steps):
        got = trade(send)
        part = pl.pallas_call(
            functools.partial(scores_kernel, step, place_of),
            out_shape=jax.ShapeDtypeStruct((classes, samples), jnp.float32),
            in_specs=[SM] * 4 + [VM, in_hbm], out_specs=VM, compiler_params=SLOTS,
            scratch_shapes=tile_room, name="scores",
        )(*scalars, got, tiles)
        residual, loss = classify(step, n_cols, part, labels)
        if owned % 128 != 0:
            start = lax.axis_index("cols") * owned
            loss = lax.dynamic_slice_in_dim(loss, start, owned, axis=1)
        losses.append(loss)
        grads = pl.pallas_call(
            functools.partial(grads_kernel, step, place_of),
            out_shape=packed,
            in_specs=[SM] * 4 + [VM, in_hbm], out_specs=VM, compiler_params=SLOTS,
            scratch_shapes=[pltpu.VMEM((entries, classes, size), jnp.float32), *tile_room],
            name="grads",
        )(*scalars, residual, tiles)
        grads = trade(grads)
        shape = jax.ShapeDtypeStruct(current.shape, current.dtype)
        more = step + 1 < steps
        current, *send = pl.pallas_call(
            functools.partial(apply_pack_kernel if more else apply_kernel, size, step, capacity),
            out_shape=(shape, packed) if more else (shape,),
            in_specs=[SM, SM, VM, VM], out_specs=(VM, VM) if more else (VM,),
            compiler_params=LOCAL, name="apply",
        )(requests, learning_rate, current, grads)
        send = send[0] if more else None
    return current, jnp.concatenate(losses)


def per_device(
    tiles, tile_scales, tile_rows, tile_cols, tile_counts, labels, learning_rate, weights
):
    args = (tiles, tile_scales, tile_rows, tile_cols, tile_counts, labels, learning_rate, weights)
    size, slots = tiles.shape[-1], tiles.shape[3]
    n_rows, n_cols = lax.axis_size("rows"), lax.axis_size("cols")
    per_owner = weights.shape[1] // size
    full = min(per_owner, slots)
    mean = slots / n_rows
    tiers = [math.ceil(mean + spread * math.sqrt(mean)) for spread in (1.75, 2, 2.25, 2.5, 3, 4)]
    tiers = sorted({min(tier, full) for tier in tiers} | {full})
    slot_ids = jnp.arange(slots, dtype=jnp.int32)

    live = slot_ids < tile_counts[:, 0, 0, None]
    mine = jnp.where(live, tile_cols[:, 0, 0], -1)
    owner = jnp.where(live, mine // per_owner, -1)
    same = mine[:, :, None] == mine[:, None, :]
    before = slot_ids[:, None] > slot_ids[None, :]
    fresh = live & ~jnp.any(same & before, axis=-1)
    lower = (owner[:, :, None] == owner[:, None, :]) & (mine[:, None, :] < mine[:, :, None])
    rank = jnp.sum((lower & fresh[:, None, :]).astype(jnp.int32), axis=-1)
    code = jnp.where(live, owner * full + rank, 0)
    everyone = collect(jnp.where(fresh, mine * full + rank, -1), n_rows, n_cols)
    most = jnp.max(jnp.where(everyone >= 0, everyone % full, 0)) + 1

    row, col = lax.axis_index("rows"), lax.axis_index("cols")
    peers = lax.dynamic_index_in_dim(everyone, col, 0, keepdims=False)
    local = peers // full - row * per_owner
    asked = (peers >= 0) & (local >= 0) & (local < per_owner)
    order = jnp.where(asked, peers % full, -1)
    picks = order[..., None, :] == jnp.arange(full, dtype=jnp.int32)[:, None]
    wanted = jnp.sum(jnp.where(picks, local[..., None, :], 0), axis=-1)
    requests = jnp.swapaxes(wanted, 0, 1).reshape(-1, n_rows * full)

    def at_capacity(capacity, branch):
        return functools.partial(sparse_program, capacity, branch)

    branches = [at_capacity(capacity, branch) for branch, capacity in enumerate(tiers)]
    operands = (code, requests, *args)
    if len(branches) == 1:
        return branches[0](*operands)
    chosen = sum((most > tier).astype(jnp.int32) for tier in tiers[:-1])
    return lax.switch(chosen, branches, *operands)


SPILL = 12
TIERS = ((23, 14), (24, 16), (26, 18), (28, 21), (32, 26))
LEFT_RIGHT = (((1,), (1,)), ((), ()))


def teams(n_rows):
    team = n_rows // 2
    row = lax.axis_index("rows")
    half, place = row // team, lax.rem(row, team)
    mate = lambda shift: half * team + lax.rem(place + shift, team)
    other = lambda shift: (1 - half) * team + lax.rem(place + shift, team)
    return team, row, half, place, mate, other


def corners(place):
    beside = place + 1 - 2 * lax.rem(place, 2)
    return beside, lax.rem(place + 2, 4), lax.rem(beside + 2, 4)


def greet_rows(peers):
    barrier = pltpu.get_barrier_semaphore()
    for peer in peers:
        pl.semaphore_signal(barrier, inc=1, device_id={"rows": peer}, device_id_type=MESH)
    return lambda: pl.semaphore_wait(barrier, len(peers))


def mark_kernel(
    n_rows, n_cols, steps, cols_ref, count_ref, all_ref, live_ref, mine, send_sems, recv_sems, own_sem
):
    row, col = lax.axis_index("rows"), lax.axis_index("cols")
    row_peers = [lax.rem(row + shift, n_rows) for shift in range(1, n_rows)]
    col_peers = [lax.rem(col + shift, n_cols) for shift in range(1, n_cols)]
    barrier = pltpu.get_barrier_semaphore()
    for peer in row_peers:
        pl.semaphore_signal(barrier, inc=1, device_id={"rows": peer}, device_id_type=MESH)
    for peer in col_peers:
        pl.semaphore_signal(barrier, inc=1, device_id={"cols": peer}, device_id_type=MESH)
    size = mine.shape[1]
    marks = []
    slots = cols_ref.shape[1]
    ids = lax.broadcasted_iota(jnp.int32, (1, slots), 1)
    for s in range(steps):
        cols = jnp.where(ids < count_ref[s], cols_ref[s : s + 1, :], -1)
        live_ref[s : s + 1, :] = cols
        owners = lax.broadcasted_iota(jnp.int32, (n_rows, slots), 0)
        places = lax.broadcasted_iota(jnp.int32, (size, slots), 0)
        first = jnp.where(cols >> 7 == owners, 1.0, 0.0).astype(jnp.bfloat16)
        second = jnp.where((cols & 127) == places, 1.0, 0.0).astype(jnp.bfloat16)
        count = lax.dot_general(first, second, LEFT_RIGHT, preferred_element_type=jnp.float32)
        marks.append(jnp.minimum(count, 1.0))
    mine[...] = jnp.concatenate(marks, axis=0).astype(jnp.bfloat16)
    pl.semaphore_wait(barrier, n_rows + n_cols - 2)
    own = pltpu.make_async_copy(mine, all_ref.at[col, row], own_sem)
    own.start()
    copies = []
    for index, peer in enumerate(row_peers):
        copies.append(
            pltpu.make_async_remote_copy(
                src_ref=mine,
                dst_ref=all_ref.at[col, row],
                send_sem=send_sems.at[index],
                recv_sem=recv_sems.at[index],
                device_id={"rows": peer},
                device_id_type=MESH,
            )
        )
        copies[-1].start()
    onward = []

    def hand_on(shift):
        piece = all_ref.at[col, lax.rem(row + n_rows - shift, n_rows)]
        for index, peer in enumerate(col_peers):
            at = n_rows + shift * (n_cols - 1) + index
            onward.append(
                pltpu.make_async_remote_copy(
                    src_ref=mine if shift == 0 else piece,
                    dst_ref=piece,
                    send_sem=send_sems.at[at],
                    recv_sem=recv_sems.at[at],
                    device_id={"cols": peer},
                    device_id_type=MESH,
                )
            )
            onward[-1].start()

    hand_on(0)
    for index, copy in enumerate(copies):
        copy.wait_recv()
        hand_on(index + 1)
    own.wait()
    for copy in copies:
        copy.wait_send()
    for copy in onward:
        copy.wait()


def mark(tile_cols, tile_counts, n_rows, n_cols, size):
    steps = tile_cols.shape[0]
    return pl.pallas_call(
        functools.partial(mark_kernel, n_rows, n_cols, steps),
        out_shape=(
            jax.ShapeDtypeStruct((n_cols, n_rows, steps * n_rows, size), jnp.bfloat16),
            jax.ShapeDtypeStruct(tile_cols.shape, jnp.int32),
        ),
        in_specs=[VM, SM],
        out_specs=(VM, VM),
        scratch_shapes=[
            pltpu.VMEM((steps * n_rows, size), jnp.bfloat16),
            pltpu.SemaphoreType.DMA((n_rows * n_cols,)),
            pltpu.SemaphoreType.DMA((n_rows * n_cols,)),
            pltpu.SemaphoreType.DMA,
        ],
        compiler_params=pltpu.CompilerParams(collective_id=0, has_side_effects=True),
        name="mark",
    )(tile_cols, tile_counts)


def plan_kernel(
    n_rows, steps, all_hbm, cols_hbm, code_ref, list_ref, tier_ref, all_ref, cols_ref, keys,
    shared_keys, table, sems
):
    fetch = [
        pltpu.make_async_copy(all_hbm, all_ref, sems.at[0]),
        pltpu.make_async_copy(cols_hbm, cols_ref, sems.at[1]),
    ]
    for copy in fetch:
        copy.start()
    team, row, half, _, _, _ = teams(n_rows)
    col = lax.axis_index("cols")
    size = all_ref.shape[-1]
    n_cols = all_ref.shape[0]
    depth = steps * n_rows
    before = lax.broadcasted_iota(jnp.int32, (size, size), 0)
    after = lax.broadcasted_iota(jnp.int32, (size, size), 1)
    triangle = jnp.where(before < after, 1.0, 0.0).astype(jnp.bfloat16)

    def ranks(flags):
        flat = flags.reshape(-1, size).astype(jnp.bfloat16)
        return jnp.dot(flat, triangle, preferred_element_type=jnp.float32).reshape(flags.shape)

    owner = lax.rem(lax.broadcasted_iota(jnp.int32, (1, depth, size), 1), n_rows)
    table[...] = jnp.full_like(table, -1.0)
    for copy in fetch:
        copy.wait()
    most_listed, most_shared = [], []
    for part in range(2):
        needs = all_ref[:, part * team : (part + 1) * team].astype(jnp.float32)
        near = owner // team == part
        wanted = needs[:, 0]
        for index in range(1, team):
            wanted = wanted + needs[:, index]
        alone = near | (wanted < 1.5)
        listed = jnp.where(alone[:, None], needs, 0.0)
        rank = ranks(listed)
        over = jnp.where(rank >= SPILL, listed, 0.0)
        spilled = over[:, 0]
        for index in range(1, team):
            spilled = jnp.maximum(spilled, over[:, index])
        shared = jnp.where(near | ((wanted < 1.5) & (spilled < 0.5)), 0.0, 1.0)
        shared_rank = ranks(shared)
        keep = (listed > 0.5) & (near[:, None] | (rank < SPILL))
        keys[:, part * team : (part + 1) * team] = jnp.where(keep, rank, -1.0)
        shared_keys[:, part] = jnp.where(shared > 0.5, shared_rank, -1.0)
        most_listed.append(jnp.max(jnp.where(keep & near[:, None], rank, -1.0)))
        most_shared.append(jnp.max(jnp.where(shared > 0.5, shared_rank, -1.0)))
    listed = jnp.maximum(*most_listed) + 1.0
    shared = jnp.maximum(*most_shared) + 1.0
    tier = jnp.int32(0)
    for cap, shared_cap in TIERS:
        tier = tier + jnp.where((listed > cap) | (shared > shared_cap), 1, 0).astype(jnp.int32)
    tier_ref[0] = tier

    sub = lax.broadcasted_iota(jnp.int32, (n_rows, size), 0)
    slot = lax.rem(sub, team)
    n_lists = 2 * team + 1
    for s in range(steps):
        mine = pl.ds(s * n_rows + row, 1)
        for index in range(team):
            at = 2 * n_rows * s + index
            table[at : at + 1, :] = keys[col, half * team + index, mine, :]
            table[at + team : at + team + 1, :] = keys[col, (1 - half) * team + index, mine, :]
        at = 2 * n_rows * s + 2 * team
        table[at : at + 1, :] = shared_keys[col, 1 - half, mine, :]
        block = pl.ds(s * n_rows, n_rows)
        listed_key = keys[col, row, block, :]
        shared_key = shared_keys[col, half, block, :]
        kind = jnp.where(sub // team == half, slot, team + slot)
        value = (kind * size).astype(jnp.float32) + listed_key
        other = ((2 * team + slot) * size).astype(jnp.float32) + shared_key
        at = 2 * n_rows * steps + s * n_rows
        table[at : at + n_rows, :] = jnp.where(shared_key >= 0.0, other, value)
    flipped = table[...].T
    lane = after.astype(jnp.float32)
    down = before.astype(jnp.float32)
    for s in range(steps):
        for index in range(n_lists):
            at = 2 * n_rows * s + index
            hit = flipped[:, at : at + 1] == lane
            picked = jnp.sum(jnp.where(hit, down, 0.0), axis=0, keepdims=True)
            list_ref[s : s + 1, index * size : (index + 1) * size] = picked.astype(jnp.int32)
    for s in range(steps):
        cols = cols_ref[s : s + 1, :]
        chosen = jnp.zeros((size, size), jnp.float32)
        for index in range(n_rows):
            at = 2 * n_rows * steps + s * n_rows + index
            chosen = jnp.where(cols >> 7 == index, flipped[:, at : at + 1], chosen)
        code = jnp.sum(jnp.where((cols & 127) == before, chosen, 0.0), axis=0, keepdims=True)
        code_ref[s : s + 1, :] = jnp.where(cols >= 0, code, 0.0).astype(jnp.int32)


def plan(everyone, tile_cols, n_rows):
    steps, slots = tile_cols.shape
    size = everyone.shape[-1]
    lists = n_rows + 1
    return pl.pallas_call(
        functools.partial(plan_kernel, n_rows, steps),
        out_shape=(
            jax.ShapeDtypeStruct((steps, slots), jnp.int32),
            jax.ShapeDtypeStruct((steps, lists * size), jnp.int32),
            jax.ShapeDtypeStruct((1,), jnp.int32),
        ),
        in_specs=[pl.BlockSpec(memory_space=pltpu.HBM)] * 2,
        out_specs=(VM, VM, SM),
        scratch_shapes=[
            pltpu.VMEM(everyone.shape, everyone.dtype),
            pltpu.VMEM(tile_cols.shape, tile_cols.dtype),
            pltpu.VMEM(everyone.shape, jnp.float32),
            pltpu.VMEM((everyone.shape[0], 2, *everyone.shape[2:]), jnp.float32),
            pltpu.VMEM((size, size), jnp.float32),
            pltpu.SemaphoreType.DMA((2,)),
        ],
        compiler_params=pltpu.CompilerParams(vmem_limit_bytes=67_000_000),
        name="plan",
    )(everyone, tile_cols)


def split_classify_kernel(
    count, step, part_ref, labels_ref, residual_ref, loss_ref, held, send_sems, recv_sems
):
    me = lax.axis_index("cols")
    owned = loss_ref.shape[1]
    barrier = pltpu.get_barrier_semaphore()
    peers = [lax.rem(me + shift, count) for shift in range(1, count)]
    for peer in peers:
        pl.semaphore_signal(barrier, inc=1, device_id={"cols": peer}, device_id_type=MESH)
    mine = lanes(me, owned)

    def copy(index, src, dst, peer):
        return pltpu.make_async_remote_copy(
            src_ref=src,
            dst_ref=dst,
            send_sem=send_sems.at[index],
            recv_sem=recv_sems.at[index],
            device_id={"cols": peer},
            device_id_type=MESH,
        )

    pl.semaphore_wait(barrier, count - 1)
    parts = [copy(i, part_ref.at[:, lanes(peer, owned)], held.at[i], peer) for i, peer in enumerate(peers)]
    for part in parts:
        part.start()
    class_ids = lax.broadcasted_iota(jnp.int32, held.shape[1:], 0)
    onehot = (class_ids == labels_ref[step : step + 1, mine]).astype(jnp.float32)
    scores = part_ref[:, mine]
    for index, part in enumerate(parts):
        part.wait_recv()
        scores = scores + held[index]
    exp_scores = jnp.exp(scores)
    total = jnp.sum(exp_scores, axis=0, keepdims=True)
    residual_ref[:, mine] = (exp_scores / total - onehot).astype(jnp.bfloat16)
    loss_ref[...] = jnp.log(total) - jnp.sum(onehot * scores, axis=0, keepdims=True)
    shared = residual_ref.at[:, mine]
    sent = [copy(count + i, shared, shared, peer) for i, peer in enumerate(peers)]
    for part in sent:
        part.start()
    for part in parts:
        part.wait_send()
    for part in sent:
        part.wait()


def split_classify(step, n_cols, part, labels):
    classes, samples = part.shape
    owned = samples // n_cols
    return pl.pallas_call(
        functools.partial(split_classify_kernel, n_cols, step),
        out_shape=(
            jax.ShapeDtypeStruct((classes, samples), jnp.bfloat16),
            jax.ShapeDtypeStruct((1, owned), jnp.float32),
        ),
        in_specs=[VM, VM],
        out_specs=(VM, VM),
        scratch_shapes=[
            pltpu.VMEM((n_cols - 1, classes, owned), jnp.float32),
            pltpu.SemaphoreType.DMA((2 * n_cols,)),
            pltpu.SemaphoreType.DMA((2 * n_cols,)),
        ],
        compiler_params=pltpu.CompilerParams(
            collective_id=1 + step, has_side_effects=True, vmem_limit_bytes=VMEM_LIMIT
        ),
        name="classify",
    )(part, labels)


class Room:
    def __init__(self, team, listed, shared):
        self.team, self.listed, self.shared = team, listed, shared
        self.spill = team * listed
        self.common = self.spill + team * SPILL
        self.packed = self.common + shared
        self.spread = self.common + team * shared

    def near(self, index):
        return pl.ds(index * self.listed, self.listed)

    def far(self, index):
        return pl.ds(self.spill + index * SPILL, SPILL)

    def group(self, index):
        return pl.ds(self.common + index * self.shared, self.shared)

    def place(self, code, size):
        kind, rank = code // size, lax.rem(code, size)
        far = self.spill + (kind - self.team) * SPILL
        common = self.common + (kind - 2 * self.team) * self.shared
        base = jnp.where(kind < 2 * self.team, far, common)
        return jnp.where(kind < self.team, kind * self.listed, base) + rank

    def entries(self, body):
        def run(first, lists, count, start):
            @pl.loop(0, count)
            def _(index):
                for which in range(lists):
                    body(start + which * count + index, first + which, index)

        run(0, self.team, self.listed, 0)
        run(self.team, self.team, SPILL, self.spill)
        run(2 * self.team, 1, self.shared, self.common)


def pack_lists(room, step, lists_ref, weights_ref, send_ref):
    size = send_ref.shape[-1]

    def body(entry, which, index):
        where = lanes(lists_ref[step, which * size + index], size)
        send_ref[entry] = weights_ref[:, where].astype(jnp.bfloat16)

    room.entries(body)


def apply_lists(room, step, lists_ref, rate_ref, weights_ref, grads_ref, out_ref):
    size = grads_ref.shape[-1]
    out_ref[...] = weights_ref[...]
    rate = rate_ref[step]

    def body(entry, which, index):
        where = lanes(lists_ref[step, which * size + index], size)
        out_ref[:, where] -= rate * grads_ref[entry].astype(jnp.float32)

    room.entries(body)


def apply_pack_lists(room, step, lists_ref, rate_ref, weights_ref, grads_ref, out_ref, send_ref):
    apply_lists(room, step, lists_ref, rate_ref, weights_ref, grads_ref, out_ref)
    pack_lists(room, step + 1, lists_ref, out_ref, send_ref)


def row_copy(sems, index, src, dst, peer):
    return pltpu.make_async_remote_copy(
        src_ref=src,
        dst_ref=dst,
        send_sem=sems[0].at[index],
        recv_sem=sems[1].at[index],
        device_id={"rows": peer},
        device_id_type=MESH,
    )


def spread_kernel(room, n_rows, send, got_ref, send_sems, recv_sems, own_sem):
    team, _, half, place, _, other = teams(n_rows)
    sems = (send_sems, recv_sems)
    beside, across, corner = corners(place)
    entered = greet_rows([half * team + to for to in (beside, across, corner)] + [other(s) for s in range(team)])

    def to_mate(index, src, dst, mate):
        copies.append(row_copy(sems, index, src, got_ref.at[dst], half * team + mate))
        copies[-1].start()
        return copies[-1]

    copies = []
    common = pl.ds(room.common, room.shared)
    own = pltpu.make_async_copy(send.at[room.near(place)], got_ref.at[room.near(place)], own_sem)
    own.start()
    entered()
    group = row_copy(sems, 0, send.at[common], got_ref.at[room.group(place)], other(0))
    group.start()
    for shift in range(team):
        to = lax.rem(place + shift, team)
        copies.append(row_copy(
            sems, 1 + shift, send.at[room.far(to)], got_ref.at[room.far(place)], other(shift)
        ))
        copies[-1].start()
    to_mate(8, send.at[room.near(beside)], room.near(place), beside)
    to_mate(9, send.at[room.near(across)], room.near(place), across)
    group.wait_recv()
    mine = room.group(place)
    passed = to_mate(6, got_ref.at[mine], mine, across)
    to_mate(5, got_ref.at[mine], mine, beside)
    to_mate(10, send.at[room.near(corner)], room.near(place), corner)

    passed.wait_recv()
    theirs = room.group(across)
    to_mate(7, got_ref.at[theirs], theirs, beside)
    passed.wait_send()
    group.wait_send()
    own.wait()
    for copy in copies:
        if copy is not passed:
            copy.wait()


def gather_kernel(
    room, n_rows, grads_ref, out_ref, pool, passing, total, send_sems, recv_sems, own_sem
):
    team, _, half, place, _, other = teams(n_rows)
    sems = (send_sems, recv_sems)
    beside, across, corner = corners(place)
    entered = greet_rows([half * team + to for to in (beside, across, corner)] + [other(s) for s in range(team)])
    own = pltpu.make_async_copy(grads_ref.at[room.near(place)], out_ref.at[room.near(place)], own_sem)
    own.start()
    entered()

    def to_mate(index, src, dst, mate):
        copy = row_copy(sems, index, src, dst, half * team + mate)
        copy.start()
        return copy

    def near(index, to):
        copies.append(to_mate(index, grads_ref.at[room.near(to)], out_ref.at[room.near(place)], to))

    copies = []
    onward = to_mate(6, grads_ref.at[room.group(corner)], pool.at[0], beside)
    direct = to_mate(5, grads_ref.at[room.group(beside)], pool.at[1], beside)
    for shift in range(team):
        to = lax.rem(place + shift, team)
        copies.append(row_copy(
            sems, 1 + shift, grads_ref.at[room.far(to)], out_ref.at[room.far(place)], other(shift)
        ))
        copies[-1].start()
    near(8, beside)
    near(9, across)
    onward.wait_recv()

    def add(first, parts, into):
        @pl.loop(0, room.shared)
        def _(index):
            value = grads_ref[first + index].astype(jnp.float32)
            for part in parts:
                value = value + pool[part, index].astype(jnp.float32)
            into[index] = value.astype(jnp.bfloat16)

    add(room.common + across * room.shared, (0,), passing)
    passed = to_mate(7, passing, pool.at[2], across)
    direct.wait_recv()
    passed.wait_recv()
    add(room.common + place * room.shared, (1, 2), total)
    common = pl.ds(room.common, room.shared)
    group = row_copy(sems, 0, total, out_ref.at[common], other(0))
    group.start()
    near(10, corner)
    for copy in (onward, direct, passed):
        copy.wait_send()
    own.wait()
    for copy in copies:
        copy.wait()
    group.wait()


def remote_sems(count):
    return [pltpu.SemaphoreType.DMA((count,)), pltpu.SemaphoreType.DMA((count,)), pltpu.SemaphoreType.DMA]


def team_program(
    n_rows, listed, shared, branch, code, lists,
    tiles, tile_scales, tile_rows, tile_cols, tile_counts, labels, learning_rate, weights
):
    classes = weights.shape[0]
    size = tiles.shape[-1]
    steps, slots = tiles.shape[0], tiles.shape[3]
    n_cols = lax.axis_size("cols")
    samples = labels.shape[1]
    owned = samples // n_cols
    room = Room(n_rows // 2, listed, shared)
    packed = jax.ShapeDtypeStruct((room.packed, classes, size), jnp.bfloat16)
    spread = jax.ShapeDtypeStruct((room.spread, classes, size), jnp.bfloat16)
    scalars = (code, tile_rows, tile_scales, tile_counts)
    in_hbm = pl.BlockSpec(memory_space=pltpu.HBM)
    tile_room = [pltpu.VMEM(tiles.shape[3:], tiles.dtype), pltpu.SemaphoreType.DMA((slots // GROUP,))]

    def remote(index):
        return pltpu.CompilerParams(
            collective_id=1 + steps + 2 * branch + index, has_side_effects=True,
            vmem_limit_bytes=VMEM_LIMIT,
        )

    current = weights
    send = pl.pallas_call(
        functools.partial(pack_lists, room, 0),
        out_shape=packed, in_specs=[SM, VM], out_specs=VM, compiler_params=LOCAL, name="pack",
    )(lists, current)
    losses = []
    for step in range(steps):
        got = pl.pallas_call(
            functools.partial(spread_kernel, room, n_rows),
            out_shape=spread, in_specs=[VM], out_specs=VM, compiler_params=remote(0),
            scratch_shapes=remote_sems(11), name="spread",
        )(send)
        part = pl.pallas_call(
            functools.partial(scores_kernel, step, lambda x: room.place(x, size)),
            out_shape=jax.ShapeDtypeStruct((classes, samples), jnp.float32),
            in_specs=[SM] * 4 + [VM, in_hbm], out_specs=VM, compiler_params=SLOTS,
            scratch_shapes=tile_room, name="scores",
        )(*scalars, got, tiles)
        residual, loss = split_classify(step, n_cols, part, labels)
        losses.append(loss)
        grads = pl.pallas_call(
            functools.partial(grads_kernel, step, lambda x: room.place(x, size)),
            out_shape=spread,
            in_specs=[SM] * 4 + [VM, in_hbm], out_specs=VM, compiler_params=SLOTS,
            scratch_shapes=[pltpu.VMEM((room.spread, classes, size), jnp.float32), *tile_room],
            name="grads",
        )(*scalars, residual, tiles)
        grads = pl.pallas_call(
            functools.partial(gather_kernel, room, n_rows),
            out_shape=packed, in_specs=[VM], out_specs=VM, compiler_params=remote(1),
            scratch_shapes=[
                pltpu.VMEM((3, shared, classes, size), jnp.bfloat16),
                pltpu.VMEM((shared, classes, size), jnp.bfloat16),
                pltpu.VMEM((shared, classes, size), jnp.bfloat16),
                *remote_sems(11),
            ],
            name="gather",
        )(grads)
        shape = jax.ShapeDtypeStruct(current.shape, current.dtype)
        more = step + 1 < steps
        current, *send = pl.pallas_call(
            functools.partial(apply_pack_lists if more else apply_lists, room, step),
            out_shape=(shape, packed) if more else (shape,),
            in_specs=[SM, SM, VM, VM], out_specs=(VM, VM) if more else (VM,),
            compiler_params=LOCAL, name="apply",
        )(lists, learning_rate, current, grads)
        send = send[0] if more else None
    return current, jnp.concatenate(losses)


def team_device(
    tiles, tile_scales, tile_rows, tile_cols, tile_counts, labels, learning_rate, weights
):
    args = (tiles, tile_scales, tile_rows, tile_cols, tile_counts, labels, learning_rate, weights)
    size = tiles.shape[-1]
    n_rows, n_cols = lax.axis_size("rows"), lax.axis_size("cols")
    cols = tile_cols[:, 0, 0]
    counts = tile_counts[:, 0, 0]
    everyone, live = mark(cols, counts, n_rows, n_cols, size)
    code, lists, tier = plan(everyone, live, n_rows)
    args = (*args[:4], counts, *args[5:])
    branches = [
        functools.partial(team_program, n_rows, listed, shared, branch)
        for branch, (listed, shared) in enumerate((*TIERS, (size, size)))
    ]
    return lax.switch(tier[0], branches, code, lists, *args)


def either_device(*args):
    tiles, weights, labels = args[0], args[-1], args[5]
    n_rows, n_cols = lax.axis_size("rows"), lax.axis_size("cols")
    size, steps = tiles.shape[-1], tiles.shape[0]
    even = n_rows == 8 and steps * n_rows * 3 <= size and labels.shape[1] // n_cols % size == 0
    if even and size == 128 and weights.shape[1] == size * size:
        return team_device(*args)
    return per_device(*args)


def solution(mesh):
    return jax.shard_map(
        either_device,
        mesh=mesh,
        in_specs=(
            P(None, "rows", "cols", None, None, None),
            P(None, "rows", "cols", None),
            P(None, "rows", "cols", None),
            P(None, "rows", "cols", None),
            P(None, "rows", "cols"),
            P(None, "rows"),
            P(),
            P(None, ("cols", "rows")),
        ),
        out_specs=(P(None, ("cols", "rows")), P(None, ("rows", "cols"))),
        check_vma=False,
    )
```

```python
import functools
import math
import jax
import jax.numpy as jnp
from jax import lax
from jax.experimental import pallas as pl
from jax.experimental.pallas import tpu as pltpu
from jax.sharding import PartitionSpec as P

MESH = pl.DeviceIdType.MESH
VMEM_LIMIT = 48 * 1024 * 1024
VM = pl.BlockSpec(memory_space=pltpu.VMEM)
SM = pl.BlockSpec(memory_space=pltpu.SMEM)
LOCAL = pltpu.CompilerParams(vmem_limit_bytes=VMEM_LIMIT)
SLOTS = pltpu.CompilerParams(vmem_limit_bytes=48 * 1024 * 1024)


def lanes(block, size):
    return pl.ds(pl.multiple_of(block * size, size), size)


def pack_body(size, step, capacity, requests_ref, weights_ref, send_ref):
    owners = send_ref.shape[0] // capacity
    full = requests_ref.shape[1] // owners

    @pl.loop(0, capacity)
    def _(index):
        for peer in range(owners):
            where = lanes(requests_ref[step, peer * full + index], size)
            send_ref[peer * capacity + index] = weights_ref[:, where].astype(jnp.bfloat16)


def apply_body(size, step, capacity, requests_ref, rate_ref, weights_ref, grads_ref, out_ref):
    owners = grads_ref.shape[0] // capacity
    full = requests_ref.shape[1] // owners
    out_ref[...] = weights_ref[...]
    rate = rate_ref[step]

    @pl.loop(0, capacity)
    def _(index):
        for peer in range(owners):
            where = lanes(requests_ref[step, peer * full + index], size)
            grad = grads_ref[peer * capacity + index].astype(jnp.float32)
            out_ref[:, where] -= rate * grad


def apply_kernel(size, step, capacity, requests_ref, rate_ref, weights_ref, grads_ref, out_ref):
    apply_body(size, step, capacity, requests_ref, rate_ref, weights_ref, grads_ref, out_ref)


def apply_pack_kernel(
    size, step, capacity, requests_ref, rate_ref, weights_ref, grads_ref, out_ref, send_ref
):
    apply_body(size, step, capacity, requests_ref, rate_ref, weights_ref, grads_ref, out_ref)
    pack_body(size, step + 1, capacity, requests_ref, out_ref, send_ref)


def exchange_kernel(axis, count, send_ref, recv_ref, send_sems, recv_sems, own_sem):
    me = lax.axis_index(axis)
    barrier = pltpu.get_barrier_semaphore()
    for shift in range(1, count):
        peer = lax.rem(me + shift, count)
        pl.semaphore_signal(barrier, inc=1, device_id={axis: peer}, device_id_type=MESH)
    own = pltpu.make_async_copy(send_ref.at[me], recv_ref.at[me], own_sem)
    own.start()
    pl.semaphore_wait(barrier, count - 1)
    copies = []
    for shift in sorted(range(1, count), key=lambda shift: abs(2 * shift - count)):
        peer = lax.rem(me + shift, count)
        copy = pltpu.make_async_remote_copy(
            src_ref=send_ref.at[peer],
            dst_ref=recv_ref.at[me],
            send_sem=send_sems.at[shift],
            recv_sem=recv_sems.at[shift],
            device_id={axis: peer},
            device_id_type=MESH,
        )
        copy.start()
        copies.append(copy)
    own.wait()
    for copy in copies:
        copy.wait()


def exchange(send, axis, count, collective_id):
    return pl.pallas_call(
        functools.partial(exchange_kernel, axis, count),
        out_shape=jax.ShapeDtypeStruct(send.shape, send.dtype),
        in_specs=[VM],
        out_specs=VM,
        scratch_shapes=[
            pltpu.SemaphoreType.DMA((count,)),
            pltpu.SemaphoreType.DMA((count,)),
            pltpu.SemaphoreType.DMA,
        ],
        compiler_params=pltpu.CompilerParams(
            collective_id=collective_id, has_side_effects=True, vmem_limit_bytes=VMEM_LIMIT
        ),
        name="exchange",
    )(send)


def collect_kernel(n_rows, n_cols, mine_ref, all_ref, send_sems, recv_sems, own_sem):
    row, col = lax.axis_index("rows"), lax.axis_index("cols")
    row_peers = [lax.rem(row + shift, n_rows) for shift in range(1, n_rows)]
    col_peers = [lax.rem(col + shift, n_cols) for shift in range(1, n_cols)]
    barrier = pltpu.get_barrier_semaphore()
    for peer in row_peers:
        pl.semaphore_signal(barrier, inc=1, device_id={"rows": peer}, device_id_type=MESH)
    for peer in col_peers:
        pl.semaphore_signal(barrier, inc=1, device_id={"cols": peer}, device_id_type=MESH)
    own = pltpu.make_async_copy(mine_ref, all_ref.at[col, row], own_sem)
    own.start()
    pl.semaphore_wait(barrier, n_rows + n_cols - 2)
    copies = []
    for index, peer in enumerate(row_peers):
        copies.append(
            pltpu.make_async_remote_copy(
                src_ref=mine_ref,
                dst_ref=all_ref.at[col, row],
                send_sem=send_sems.at[index],
                recv_sem=recv_sems.at[index],
                device_id={"rows": peer},
                device_id_type=MESH,
            )
        )
        copies[-1].start()
    own.wait()
    for copy in copies:
        copy.wait()
    copies = []
    for index, peer in enumerate(col_peers):
        copies.append(
            pltpu.make_async_remote_copy(
                src_ref=all_ref.at[col],
                dst_ref=all_ref.at[col],
                send_sem=send_sems.at[n_rows + index],
                recv_sem=recv_sems.at[n_rows + index],
                device_id={"cols": peer},
                device_id_type=MESH,
            )
        )
        copies[-1].start()
    for copy in copies:
        copy.wait()


def collect(mine, n_rows, n_cols):
    return pl.pallas_call(
        functools.partial(collect_kernel, n_rows, n_cols),
        out_shape=jax.ShapeDtypeStruct((n_cols, n_rows, *mine.shape), mine.dtype),
        in_specs=[VM],
        out_specs=VM,
        scratch_shapes=[
            pltpu.SemaphoreType.DMA((n_rows + n_cols,)),
            pltpu.SemaphoreType.DMA((n_rows + n_cols,)),
            pltpu.SemaphoreType.DMA,
        ],
        compiler_params=pltpu.CompilerParams(collective_id=0, has_side_effects=True),
        name="collect",
    )(mine)


GROUP = 16


def slot_scalars(step, place_of, slot, code_ref, row_ref, scale_ref, count_ref):
    place = place_of(code_ref[step, slot])
    count = count_ref[(step,) + (0,) * (len(count_ref.shape) - 1)]
    factor = jnp.where(slot < count, scale_ref[step, 0, 0, slot], 0.0)
    return place, row_ref[step, 0, 0, slot], factor


def fetch_tiles(step, tiles_ref, held_ref, sems):
    if sems is None:
        return lambda group: None

    def copy(group):
        part = pl.ds(group * GROUP, GROUP)
        return pltpu.make_async_copy(
            tiles_ref.at[step, 0, 0, part], held_ref.at[part], sems.at[group]
        )

    for group in range(held_ref.shape[0] // GROUP):
        copy(group).start()
    return lambda group: copy(group).wait()


def scores_kernel(
    step, place_of, code_ref, row_ref, scale_ref, count_ref, recv_ref, tiles_ref, out_ref,
    held_ref, sems,
):
    size = held_ref.shape[-1]
    arrived = fetch_tiles(step, tiles_ref, held_ref, sems)
    out_ref[...] = jnp.zeros_like(out_ref)

    @pl.loop(0, held_ref.shape[0] // GROUP)
    def _(group):
        arrived(group)
        products = []
        for lane in range(GROUP):
            slot = group * GROUP + lane
            place, row, factor = slot_scalars(
                step, place_of, slot, code_ref, row_ref, scale_ref, count_ref
            )
            product = lax.dot_general(
                recv_ref[place],
                held_ref[slot],
                (((1,), (1,)), ((), ())),
                preferred_element_type=jnp.float32,
            )
            products.append((row, product * factor))
        for row, product in products:
            out_ref[:, lanes(row, size)] += product


def classify_kernel(
    axis, count, step, part_ref, labels_ref, residual_ref, loss_ref, held, losses, send_sems,
    recv_sems,
):
    me = lax.axis_index(axis)
    barrier = pltpu.get_barrier_semaphore()
    for shift in range(1, count):
        peer = lax.rem(me + shift, count)
        pl.semaphore_signal(barrier, inc=1, device_id={axis: peer}, device_id_type=MESH)
    pl.semaphore_wait(barrier, count - 1)
    copies = []
    for shift in range(1, count):
        peer = lax.rem(me + shift, count)
        copy = pltpu.make_async_remote_copy(
            src_ref=part_ref,
            dst_ref=held.at[shift],
            send_sem=send_sems.at[shift],
            recv_sem=recv_sems.at[shift],
            device_id={axis: peer},
            device_id_type=MESH,
        )
        copy.start()
        copies.append(copy)
    scores = part_ref[...]
    for shift, copy in enumerate(copies):
        copy.wait()
        scores = scores + held[shift + 1]
    exp_scores = jnp.exp(scores)
    total = jnp.sum(exp_scores, axis=0, keepdims=True)
    class_ids = lax.broadcasted_iota(jnp.int32, scores.shape, 0)
    onehot = (class_ids == labels_ref[step : step + 1, :]).astype(jnp.float32)
    losses[...] = jnp.log(total) - jnp.sum(onehot * scores, axis=0, keepdims=True)
    if loss_ref.shape == losses.shape:
        loss_ref[...] = losses[...]
    else:
        loss_ref[...] = losses[:, lanes(me, loss_ref.shape[1])]
    residual_ref[...] = (exp_scores / total - onehot).astype(jnp.bfloat16)


def classify(step, n_cols, part, labels):
    classes, samples = part.shape
    owned = samples // n_cols
    return pl.pallas_call(
        functools.partial(classify_kernel, "cols", n_cols, step),
        out_shape=(
            jax.ShapeDtypeStruct((classes, samples), jnp.bfloat16),
            jax.ShapeDtypeStruct((1, owned if owned % 128 == 0 else samples), jnp.float32),
        ),
        in_specs=[VM, VM],
        out_specs=(VM, VM),
        scratch_shapes=[
            pltpu.VMEM((n_cols, classes, samples), jnp.float32),
            pltpu.VMEM((1, samples), jnp.float32),
            pltpu.SemaphoreType.DMA((n_cols,)),
            pltpu.SemaphoreType.DMA((n_cols,)),
        ],
        compiler_params=pltpu.CompilerParams(collective_id=1 + step, has_side_effects=True),
        name="classify",
    )(part, labels)


def grads_kernel(
    step, place_of, code_ref, row_ref, scale_ref, count_ref, residual_ref, tiles_ref,
    out_ref, total, held_ref, sems,
):
    size = held_ref.shape[-1]
    arrived = fetch_tiles(step, tiles_ref, held_ref, sems)
    total[...] = jnp.zeros_like(total)

    @pl.loop(0, held_ref.shape[0] // GROUP)
    def _(group):
        arrived(group)
        products = []
        for lane in range(GROUP):
            slot = group * GROUP + lane
            place, row, factor = slot_scalars(
                step, place_of, slot, code_ref, row_ref, scale_ref, count_ref
            )
            product = jnp.dot(
                residual_ref[:, lanes(row, size)],
                held_ref[slot],
                preferred_element_type=jnp.float32,
            )
            products.append((place, product * factor))
        for place, product in products:
            total[place] += product

    out_ref[...] = total[...].astype(jnp.bfloat16)


def sparse_program(
    capacity, branch, code, requests,
    tiles, tile_scales, tile_rows, tile_cols, tile_counts, labels, learning_rate, weights
):
    classes = weights.shape[0]
    size = tiles.shape[-1]
    steps = tiles.shape[0]
    n_rows, n_cols = lax.axis_size("rows"), lax.axis_size("cols")
    full = requests.shape[1] // n_rows
    samples = labels.shape[1]
    entries = n_rows * capacity
    packed = jax.ShapeDtypeStruct((entries, classes, size), jnp.bfloat16)
    owned = samples // n_cols
    scalars = (code, tile_rows, tile_scales, tile_counts)
    trade_id = 1 + steps + branch
    slots = tiles.shape[3]
    in_hbm = pl.BlockSpec(memory_space=pltpu.HBM)
    tile_room = [pltpu.VMEM(tiles.shape[3:], tiles.dtype), pltpu.SemaphoreType.DMA((slots // GROUP,))]

    def place_of(x):
        return x // full * capacity + lax.rem(x, full)

    def trade(x):
        blocks = x.reshape(n_rows, capacity, classes, size)
        return exchange(blocks, "rows", n_rows, trade_id).reshape(packed.shape)

    current = weights
    send = pl.pallas_call(
        functools.partial(pack_body, size, 0, capacity),
        out_shape=packed, in_specs=[SM, VM], out_specs=VM, compiler_params=LOCAL, name="pack",
    )(requests, current)
    losses = []
    for step in range(steps):
        got = trade(send)
        part = pl.pallas_call(
            functools.partial(scores_kernel, step, place_of),
            out_shape=jax.ShapeDtypeStruct((classes, samples), jnp.float32),
            in_specs=[SM] * 4 + [VM, in_hbm], out_specs=VM, compiler_params=SLOTS,
            scratch_shapes=tile_room, name="scores",
        )(*scalars, got, tiles)
        residual, loss = classify(step, n_cols, part, labels)
        if owned % 128 != 0:
            start = lax.axis_index("cols") * owned
            loss = lax.dynamic_slice_in_dim(loss, start, owned, axis=1)
        losses.append(loss)
        grads = pl.pallas_call(
            functools.partial(grads_kernel, step, place_of),
            out_shape=packed,
            in_specs=[SM] * 4 + [VM, in_hbm], out_specs=VM, compiler_params=SLOTS,
            scratch_shapes=[pltpu.VMEM((entries, classes, size), jnp.float32), *tile_room],
            name="grads",
        )(*scalars, residual, tiles)
        grads = trade(grads)
        shape = jax.ShapeDtypeStruct(current.shape, current.dtype)
        more = step + 1 < steps
        current, *send = pl.pallas_call(
            functools.partial(apply_pack_kernel if more else apply_kernel, size, step, capacity),
            out_shape=(shape, packed) if more else (shape,),
            in_specs=[SM, SM, VM, VM], out_specs=(VM, VM) if more else (VM,),
            compiler_params=LOCAL, name="apply",
        )(requests, learning_rate, current, grads)
        send = send[0] if more else None
    return current, jnp.concatenate(losses)


def per_device(
    tiles, tile_scales, tile_rows, tile_cols, tile_counts, labels, learning_rate, weights
):
    args = (tiles, tile_scales, tile_rows, tile_cols, tile_counts, labels, learning_rate, weights)
    size, slots = tiles.shape[-1], tiles.shape[3]
    n_rows, n_cols = lax.axis_size("rows"), lax.axis_size("cols")
    per_owner = weights.shape[1] // size
    full = min(per_owner, slots)
    mean = slots / n_rows
    tiers = [math.ceil(mean + spread * math.sqrt(mean)) for spread in (1.75, 2, 2.25, 2.5, 3, 4)]
    tiers = sorted({min(tier, full) for tier in tiers} | {full})
    slot_ids = jnp.arange(slots, dtype=jnp.int32)

    live = slot_ids < tile_counts[:, 0, 0, None]
    mine = jnp.where(live, tile_cols[:, 0, 0], -1)
    owner = jnp.where(live, mine // per_owner, -1)
    same = mine[:, :, None] == mine[:, None, :]
    before = slot_ids[:, None] > slot_ids[None, :]
    fresh = live & ~jnp.any(same & before, axis=-1)
    lower = (owner[:, :, None] == owner[:, None, :]) & (mine[:, None, :] < mine[:, :, None])
    rank = jnp.sum((lower & fresh[:, None, :]).astype(jnp.int32), axis=-1)
    code = jnp.where(live, owner * full + rank, 0)
    everyone = collect(jnp.where(fresh, mine * full + rank, -1), n_rows, n_cols)
    most = jnp.max(jnp.where(everyone >= 0, everyone % full, 0)) + 1

    row, col = lax.axis_index("rows"), lax.axis_index("cols")
    peers = lax.dynamic_index_in_dim(everyone, col, 0, keepdims=False)
    local = peers // full - row * per_owner
    asked = (peers >= 0) & (local >= 0) & (local < per_owner)
    order = jnp.where(asked, peers % full, -1)
    picks = order[..., None, :] == jnp.arange(full, dtype=jnp.int32)[:, None]
    wanted = jnp.sum(jnp.where(picks, local[..., None, :], 0), axis=-1)
    requests = jnp.swapaxes(wanted, 0, 1).reshape(-1, n_rows * full)

    def at_capacity(capacity, branch):
        return functools.partial(sparse_program, capacity, branch)

    branches = [at_capacity(capacity, branch) for branch, capacity in enumerate(tiers)]
    operands = (code, requests, *args)
    if len(branches) == 1:
        return branches[0](*operands)
    chosen = sum((most > tier).astype(jnp.int32) for tier in tiers[:-1])
    return lax.switch(chosen, branches, *operands)


SPILL = 12
TIERS = ((23, 14), (24, 16), (26, 18), (28, 21), (32, 26))
LEFT_RIGHT = (((1,), (1,)), ((), ()))


def teams(n_rows):
    team = n_rows // 2
    row = lax.axis_index("rows")
    half, place = row // team, lax.rem(row, team)
    mate = lambda shift: half * team + lax.rem(place + shift, team)
    other = lambda shift: (1 - half) * team + lax.rem(place + shift, team)
    return team, row, half, place, mate, other


def corners(place):
    beside = place + 1 - 2 * lax.rem(place, 2)
    return beside, lax.rem(place + 2, 4), lax.rem(beside + 2, 4)


def greet_rows(peers):
    barrier = pltpu.get_barrier_semaphore()
    for peer in peers:
        pl.semaphore_signal(barrier, inc=1, device_id={"rows": peer}, device_id_type=MESH)
    return lambda: pl.semaphore_wait(barrier, len(peers))


def mark_kernel(
    n_rows, n_cols, steps, cols_ref, count_ref, all_ref, live_ref, mine, send_sems, recv_sems, own_sem
):
    row, col = lax.axis_index("rows"), lax.axis_index("cols")
    row_peers = [lax.rem(row + shift, n_rows) for shift in range(1, n_rows)]
    col_peers = [lax.rem(col + shift, n_cols) for shift in range(1, n_cols)]
    barrier = pltpu.get_barrier_semaphore()
    for peer in row_peers:
        pl.semaphore_signal(barrier, inc=1, device_id={"rows": peer}, device_id_type=MESH)
    for peer in col_peers:
        pl.semaphore_signal(barrier, inc=1, device_id={"cols": peer}, device_id_type=MESH)
    size = mine.shape[1]
    marks = []
    slots = cols_ref.shape[1]
    ids = lax.broadcasted_iota(jnp.int32, (1, slots), 1)
    for s in range(steps):
        cols = jnp.where(ids < count_ref[s], cols_ref[s : s + 1, :], -1)
        live_ref[s : s + 1, :] = cols
        owners = lax.broadcasted_iota(jnp.int32, (n_rows, slots), 0)
        places = lax.broadcasted_iota(jnp.int32, (size, slots), 0)
        first = jnp.where(cols >> 7 == owners, 1.0, 0.0).astype(jnp.bfloat16)
        second = jnp.where((cols & 127) == places, 1.0, 0.0).astype(jnp.bfloat16)
        count = lax.dot_general(first, second, LEFT_RIGHT, preferred_element_type=jnp.float32)
        marks.append(jnp.minimum(count, 1.0))
    mine[...] = jnp.concatenate(marks, axis=0).astype(jnp.bfloat16)
    pl.semaphore_wait(barrier, n_rows + n_cols - 2)
    own = pltpu.make_async_copy(mine, all_ref.at[col, row], own_sem)
    own.start()
    copies = []
    for index, peer in enumerate(row_peers):
        copies.append(
            pltpu.make_async_remote_copy(
                src_ref=mine,
                dst_ref=all_ref.at[col, row],
                send_sem=send_sems.at[index],
                recv_sem=recv_sems.at[index],
                device_id={"rows": peer},
                device_id_type=MESH,
            )
        )
        copies[-1].start()
    onward = []

    def hand_on(shift):
        piece = all_ref.at[col, lax.rem(row + n_rows - shift, n_rows)]
        for index, peer in enumerate(col_peers):
            at = n_rows + shift * (n_cols - 1) + index
            onward.append(
                pltpu.make_async_remote_copy(
                    src_ref=mine if shift == 0 else piece,
                    dst_ref=piece,
                    send_sem=send_sems.at[at],
                    recv_sem=recv_sems.at[at],
                    device_id={"cols": peer},
                    device_id_type=MESH,
                )
            )
            onward[-1].start()

    hand_on(0)
    for index, copy in enumerate(copies):
        copy.wait_recv()
        hand_on(index + 1)
    own.wait()
    for copy in copies:
        copy.wait_send()
    for copy in onward:
        copy.wait()


def mark(tile_cols, tile_counts, n_rows, n_cols, size):
    steps = tile_cols.shape[0]
    return pl.pallas_call(
        functools.partial(mark_kernel, n_rows, n_cols, steps),
        out_shape=(
            jax.ShapeDtypeStruct((n_cols, n_rows, steps * n_rows, size), jnp.bfloat16),
            jax.ShapeDtypeStruct(tile_cols.shape, jnp.int32),
        ),
        in_specs=[VM, SM],
        out_specs=(VM, VM),
        scratch_shapes=[
            pltpu.VMEM((steps * n_rows, size), jnp.bfloat16),
            pltpu.SemaphoreType.DMA((n_rows * n_cols,)),
            pltpu.SemaphoreType.DMA((n_rows * n_cols,)),
            pltpu.SemaphoreType.DMA,
        ],
        compiler_params=pltpu.CompilerParams(collective_id=0, has_side_effects=True),
        name="mark",
    )(tile_cols, tile_counts)


def plan_kernel(
    n_rows, steps, all_hbm, cols_hbm, code_ref, list_ref, tier_ref, all_ref, cols_ref, keys,
    shared_keys, table, sems
):
    fetch = [
        pltpu.make_async_copy(all_hbm, all_ref, sems.at[0]),
        pltpu.make_async_copy(cols_hbm, cols_ref, sems.at[1]),
    ]
    for copy in fetch:
        copy.start()
    team, row, half, _, _, _ = teams(n_rows)
    col = lax.axis_index("cols")
    size = all_ref.shape[-1]
    n_cols = all_ref.shape[0]
    depth = steps * n_rows
    before = lax.broadcasted_iota(jnp.int32, (size, size), 0)
    after = lax.broadcasted_iota(jnp.int32, (size, size), 1)
    triangle = jnp.where(before < after, 1.0, 0.0).astype(jnp.bfloat16)

    def ranks(flags):
        flat = flags.reshape(-1, size).astype(jnp.bfloat16)
        return jnp.dot(flat, triangle, preferred_element_type=jnp.float32).reshape(flags.shape)

    owner = lax.rem(lax.broadcasted_iota(jnp.int32, (1, depth, size), 1), n_rows)
    table[...] = jnp.full_like(table, -1.0)
    for copy in fetch:
        copy.wait()
    most_listed, most_shared = [], []
    for part in range(2):
        needs = all_ref[:, part * team : (part + 1) * team].astype(jnp.float32)
        near = owner // team == part
        wanted = needs[:, 0]
        for index in range(1, team):
            wanted = wanted + needs[:, index]
        alone = near | (wanted < 1.5)
        listed = jnp.where(alone[:, None], needs, 0.0)
        rank = ranks(listed)
        over = jnp.where(rank >= SPILL, listed, 0.0)
        spilled = over[:, 0]
        for index in range(1, team):
            spilled = jnp.maximum(spilled, over[:, index])
        shared = jnp.where(near | ((wanted < 1.5) & (spilled < 0.5)), 0.0, 1.0)
        shared_rank = ranks(shared)
        keep = (listed > 0.5) & (near[:, None] | (rank < SPILL))
        keys[:, part * team : (part + 1) * team] = jnp.where(keep, rank, -1.0)
        shared_keys[:, part] = jnp.where(shared > 0.5, shared_rank, -1.0)
        most_listed.append(jnp.max(jnp.where(keep & near[:, None], rank, -1.0)))
        most_shared.append(jnp.max(jnp.where(shared > 0.5, shared_rank, -1.0)))
    listed = jnp.maximum(*most_listed) + 1.0
    shared = jnp.maximum(*most_shared) + 1.0
    tier = jnp.int32(0)
    for cap, shared_cap in TIERS:
        tier = tier + jnp.where((listed > cap) | (shared > shared_cap), 1, 0).astype(jnp.int32)
    tier_ref[0] = tier

    sub = lax.broadcasted_iota(jnp.int32, (n_rows, size), 0)
    slot = lax.rem(sub, team)
    n_lists = 2 * team + 1
    for s in range(steps):
        mine = pl.ds(s * n_rows + row, 1)
        for index in range(team):
            at = 2 * n_rows * s + index
            table[at : at + 1, :] = keys[col, half * team + index, mine, :]
            table[at + team : at + team + 1, :] = keys[col, (1 - half) * team + index, mine, :]
        at = 2 * n_rows * s + 2 * team
        table[at : at + 1, :] = shared_keys[col, 1 - half, mine, :]
        block = pl.ds(s * n_rows, n_rows)
        listed_key = keys[col, row, block, :]
        shared_key = shared_keys[col, half, block, :]
        kind = jnp.where(sub // team == half, slot, team + slot)
        value = (kind * size).astype(jnp.float32) + listed_key
        other = ((2 * team + slot) * size).astype(jnp.float32) + shared_key
        at = 2 * n_rows * steps + s * n_rows
        table[at : at + n_rows, :] = jnp.where(shared_key >= 0.0, other, value)
    flipped = table[...].T
    lane = after.astype(jnp.float32)
    down = before.astype(jnp.float32)
    for s in range(steps):
        for index in range(n_lists):
            at = 2 * n_rows * s + index
            hit = flipped[:, at : at + 1] == lane
            picked = jnp.sum(jnp.where(hit, down, 0.0), axis=0, keepdims=True)
            list_ref[s : s + 1, index * size : (index + 1) * size] = picked.astype(jnp.int32)
    for s in range(steps):
        cols = cols_ref[s : s + 1, :]
        chosen = jnp.zeros((size, size), jnp.float32)
        for index in range(n_rows):
            at = 2 * n_rows * steps + s * n_rows + index
            chosen = jnp.where(cols >> 7 == index, flipped[:, at : at + 1], chosen)
        code = jnp.sum(jnp.where((cols & 127) == before, chosen, 0.0), axis=0, keepdims=True)
        code_ref[s : s + 1, :] = jnp.where(cols >= 0, code, 0.0).astype(jnp.int32)


def plan(everyone, tile_cols, n_rows):
    steps, slots = tile_cols.shape
    size = everyone.shape[-1]
    lists = n_rows + 1
    return pl.pallas_call(
        functools.partial(plan_kernel, n_rows, steps),
        out_shape=(
            jax.ShapeDtypeStruct((steps, slots), jnp.int32),
            jax.ShapeDtypeStruct((steps, lists * size), jnp.int32),
            jax.ShapeDtypeStruct((1,), jnp.int32),
        ),
        in_specs=[pl.BlockSpec(memory_space=pltpu.HBM)] * 2,
        out_specs=(VM, VM, SM),
        scratch_shapes=[
            pltpu.VMEM(everyone.shape, everyone.dtype),
            pltpu.VMEM(tile_cols.shape, tile_cols.dtype),
            pltpu.VMEM(everyone.shape, jnp.float32),
            pltpu.VMEM((everyone.shape[0], 2, *everyone.shape[2:]), jnp.float32),
            pltpu.VMEM((size, size), jnp.float32),
            pltpu.SemaphoreType.DMA((2,)),
        ],
        compiler_params=pltpu.CompilerParams(vmem_limit_bytes=67_000_000),
        name="plan",
    )(everyone, tile_cols)


def split_classify_kernel(
    count, step, part_ref, labels_ref, residual_ref, loss_ref, held, send_sems, recv_sems
):
    me = lax.axis_index("cols")
    owned = loss_ref.shape[1]
    barrier = pltpu.get_barrier_semaphore()
    peers = [lax.rem(me + shift, count) for shift in range(1, count)]
    for peer in peers:
        pl.semaphore_signal(barrier, inc=1, device_id={"cols": peer}, device_id_type=MESH)
    mine = lanes(me, owned)

    def copy(index, src, dst, peer):
        return pltpu.make_async_remote_copy(
            src_ref=src,
            dst_ref=dst,
            send_sem=send_sems.at[index],
            recv_sem=recv_sems.at[index],
            device_id={"cols": peer},
            device_id_type=MESH,
        )

    pl.semaphore_wait(barrier, count - 1)
    parts = [copy(i, part_ref.at[:, lanes(peer, owned)], held.at[i], peer) for i, peer in enumerate(peers)]
    for part in parts:
        part.start()
    class_ids = lax.broadcasted_iota(jnp.int32, held.shape[1:], 0)
    onehot = (class_ids == labels_ref[step : step + 1, mine]).astype(jnp.float32)
    scores = part_ref[:, mine]
    for index, part in enumerate(parts):
        part.wait_recv()
        scores = scores + held[index]
    exp_scores = jnp.exp(scores)
    total = jnp.sum(exp_scores, axis=0, keepdims=True)
    residual_ref[:, mine] = (exp_scores / total - onehot).astype(jnp.bfloat16)
    loss_ref[...] = jnp.log(total) - jnp.sum(onehot * scores, axis=0, keepdims=True)
    shared = residual_ref.at[:, mine]
    sent = [copy(count + i, shared, shared, peer) for i, peer in enumerate(peers)]
    for part in sent:
        part.start()
    for part in parts:
        part.wait_send()
    for part in sent:
        part.wait()


def split_classify(step, n_cols, part, labels):
    classes, samples = part.shape
    owned = samples // n_cols
    return pl.pallas_call(
        functools.partial(split_classify_kernel, n_cols, step),
        out_shape=(
            jax.ShapeDtypeStruct((classes, samples), jnp.bfloat16),
            jax.ShapeDtypeStruct((1, owned), jnp.float32),
        ),
        in_specs=[VM, VM],
        out_specs=(VM, VM),
        scratch_shapes=[
            pltpu.VMEM((n_cols - 1, classes, owned), jnp.float32),
            pltpu.SemaphoreType.DMA((2 * n_cols,)),
            pltpu.SemaphoreType.DMA((2 * n_cols,)),
        ],
        compiler_params=pltpu.CompilerParams(
            collective_id=1 + step, has_side_effects=True, vmem_limit_bytes=VMEM_LIMIT
        ),
        name="classify",
    )(part, labels)


class Room:
    def __init__(self, team, listed, shared):
        self.team, self.listed, self.shared = team, listed, shared
        self.spill = team * listed
        self.common = self.spill + team * SPILL
        self.packed = self.common + shared
        self.spread = self.common + team * shared
        self.limit = (16 if shared < 64 else 48) * 1024 * 1024

    def near(self, index):
        return pl.ds(index * self.listed, self.listed)

    def far(self, index):
        return pl.ds(self.spill + index * SPILL, SPILL)

    def group(self, index):
        return pl.ds(self.common + index * self.shared, self.shared)

    def place(self, code, size):
        kind, rank = code // size, lax.rem(code, size)
        far = self.spill + (kind - self.team) * SPILL
        common = self.common + (kind - 2 * self.team) * self.shared
        base = jnp.where(kind < 2 * self.team, far, common)
        return jnp.where(kind < self.team, kind * self.listed, base) + rank

    def entries(self, body):
        def run(first, lists, count, start):
            @pl.loop(0, count)
            def _(index):
                for which in range(lists):
                    body(start + which * count + index, first + which, index)

        run(0, self.team, self.listed, 0)
        run(self.team, self.team, SPILL, self.spill)
        run(2 * self.team, 1, self.shared, self.common)


def pack_lists(room, step, lists_ref, weights_ref, send_ref):
    size = send_ref.shape[-1]

    def body(entry, which, index):
        where = lanes(lists_ref[step, which * size + index], size)
        send_ref[entry] = weights_ref[:, where].astype(jnp.bfloat16)

    room.entries(body)


def apply_lists(room, step, lists_ref, rate_ref, weights_ref, grads_ref, out_ref):
    size = grads_ref.shape[-1]
    out_ref[...] = weights_ref[...]
    rate = rate_ref[step]

    def body(entry, which, index):
        where = lanes(lists_ref[step, which * size + index], size)
        out_ref[:, where] -= rate * grads_ref[entry].astype(jnp.float32)

    room.entries(body)


def apply_pack_lists(room, step, lists_ref, rate_ref, weights_ref, grads_ref, out_ref, send_ref):
    apply_lists(room, step, lists_ref, rate_ref, weights_ref, grads_ref, out_ref)
    pack_lists(room, step + 1, lists_ref, out_ref, send_ref)


def row_copy(sems, index, src, dst, peer):
    return pltpu.make_async_remote_copy(
        src_ref=src,
        dst_ref=dst,
        send_sem=sems[0].at[index],
        recv_sem=sems[1].at[index],
        device_id={"rows": peer},
        device_id_type=MESH,
    )


def spread_kernel(room, n_rows, send, got_ref, send_sems, recv_sems, own_sem):
    team, _, half, place, _, other = teams(n_rows)
    sems = (send_sems, recv_sems)
    beside, across, corner = corners(place)
    entered = greet_rows([half * team + to for to in (beside, across, corner)] + [other(s) for s in range(team)])

    def to_mate(index, src, dst, mate):
        copies.append(row_copy(sems, index, src, got_ref.at[dst], half * team + mate))
        copies[-1].start()
        return copies[-1]

    copies = []
    common = pl.ds(room.common, room.shared)
    own = pltpu.make_async_copy(send.at[room.near(place)], got_ref.at[room.near(place)], own_sem)
    own.start()
    entered()
    group = row_copy(sems, 0, send.at[common], got_ref.at[room.group(place)], other(0))
    group.start()
    for shift in range(team):
        to = lax.rem(place + shift, team)
        copies.append(row_copy(
            sems, 1 + shift, send.at[room.far(to)], got_ref.at[room.far(place)], other(shift)
        ))
        copies[-1].start()
    to_mate(8, send.at[room.near(beside)], room.near(place), beside)
    to_mate(9, send.at[room.near(across)], room.near(place), across)
    group.wait_recv()
    mine = room.group(place)
    passed = to_mate(6, got_ref.at[mine], mine, across)
    to_mate(5, got_ref.at[mine], mine, beside)
    to_mate(10, send.at[room.near(corner)], room.near(place), corner)

    passed.wait_recv()
    theirs = room.group(across)
    to_mate(7, got_ref.at[theirs], theirs, beside)
    passed.wait_send()
    group.wait_send()
    own.wait()
    for copy in copies:
        if copy is not passed:
            copy.wait()


def gather_kernel(
    room, n_rows, grads_ref, out_ref, pool, passing, total, send_sems, recv_sems, own_sem
):
    team, _, half, place, _, other = teams(n_rows)
    sems = (send_sems, recv_sems)
    beside, across, corner = corners(place)
    entered = greet_rows([half * team + to for to in (beside, across, corner)] + [other(s) for s in range(team)])
    own = pltpu.make_async_copy(grads_ref.at[room.near(place)], out_ref.at[room.near(place)], own_sem)
    own.start()
    entered()

    def to_mate(index, src, dst, mate):
        copy = row_copy(sems, index, src, dst, half * team + mate)
        copy.start()
        return copy

    def near(index, to):
        copies.append(to_mate(index, grads_ref.at[room.near(to)], out_ref.at[room.near(place)], to))

    copies = []
    onward = to_mate(6, grads_ref.at[room.group(corner)], pool.at[0], beside)
    direct = to_mate(5, grads_ref.at[room.group(beside)], pool.at[1], beside)
    for shift in range(team):
        to = lax.rem(place + shift, team)
        copies.append(row_copy(
            sems, 1 + shift, grads_ref.at[room.far(to)], out_ref.at[room.far(place)], other(shift)
        ))
        copies[-1].start()
    near(8, beside)
    near(9, across)
    onward.wait_recv()

    def add(first, parts, into):
        @pl.loop(0, room.shared)
        def _(index):
            value = grads_ref[first + index].astype(jnp.float32)
            for part in parts:
                value = value + pool[part, index].astype(jnp.float32)
            into[index] = value.astype(jnp.bfloat16)

    add(room.common + across * room.shared, (0,), passing)
    passed = to_mate(7, passing, pool.at[2], across)
    direct.wait_recv()
    passed.wait_recv()
    add(room.common + place * room.shared, (1, 2), total)
    common = pl.ds(room.common, room.shared)
    group = row_copy(sems, 0, total, out_ref.at[common], other(0))
    group.start()
    near(10, corner)
    for copy in (onward, direct, passed):
        copy.wait_send()
    own.wait()
    for copy in copies:
        copy.wait()
    group.wait()


def remote_sems(count):
    return [pltpu.SemaphoreType.DMA((count,)), pltpu.SemaphoreType.DMA((count,)), pltpu.SemaphoreType.DMA]


def resident_scores(step, place_of, code_ref, row_ref, scale_ref, count_ref, recv_ref, tiles_ref, out_ref):
    held_ref = tiles_ref.at[step, 0, 0]
    scores_kernel(
        step, place_of, code_ref, row_ref, scale_ref, count_ref, recv_ref, None, out_ref, held_ref, None
    )


def resident_grads(
    step, place_of, code_ref, row_ref, scale_ref, count_ref, residual_ref, tiles_ref, out_ref, total
):
    held_ref = tiles_ref.at[step, 0, 0]
    grads_kernel(
        step, place_of, code_ref, row_ref, scale_ref, count_ref, residual_ref, None, out_ref, total,
        held_ref, None,
    )


def team_program(
    n_rows, listed, shared, branch, code, lists,
    tiles, tile_scales, tile_rows, tile_cols, tile_counts, labels, learning_rate, weights
):
    classes = weights.shape[0]
    size = tiles.shape[-1]
    steps, slots = tiles.shape[0], tiles.shape[3]
    n_cols = lax.axis_size("cols")
    samples = labels.shape[1]
    owned = samples // n_cols
    room = Room(n_rows // 2, listed, shared)
    packed = jax.ShapeDtypeStruct((room.packed, classes, size), jnp.bfloat16)
    spread = jax.ShapeDtypeStruct((room.spread, classes, size), jnp.bfloat16)
    scalars = (code, tile_rows, tile_scales, tile_counts)
    tile_room = [pltpu.VMEM(tiles.shape[3:], tiles.dtype), pltpu.SemaphoreType.DMA((slots // GROUP,))]
    slots_params = pltpu.CompilerParams(vmem_limit_bytes=room.limit)

    def remote(index):
        return pltpu.CompilerParams(
            collective_id=1 + steps + 2 * branch + index, has_side_effects=True,
            vmem_limit_bytes=room.limit,
        )

    current = weights
    send = pl.pallas_call(
        functools.partial(pack_lists, room, 0),
        out_shape=packed, in_specs=[SM, VM], out_specs=VM, compiler_params=LOCAL, name="pack",
    )(lists, current)
    losses = []
    for step in range(steps):
        got = pl.pallas_call(
            functools.partial(spread_kernel, room, n_rows),
            out_shape=spread, in_specs=[VM], out_specs=VM, compiler_params=remote(0),
            scratch_shapes=remote_sems(11), name="spread",
        )(send)
        part = pl.pallas_call(
            functools.partial(
                resident_scores if step else scores_kernel, step, lambda x: room.place(x, size)
            ),
            out_shape=jax.ShapeDtypeStruct((classes, samples), jnp.float32),
            in_specs=[SM] * 4 + [VM, VM if step else pl.BlockSpec(memory_space=pltpu.HBM)],
            out_specs=VM, compiler_params=slots_params, name="scores",
            scratch_shapes=[] if step else tile_room,
        )(*scalars, got, tiles)
        residual, loss = split_classify(step, n_cols, part, labels)
        losses.append(loss)
        grads = pl.pallas_call(
            functools.partial(resident_grads, step, lambda x: room.place(x, size)),
            out_shape=spread,
            in_specs=[SM] * 4 + [VM, VM], out_specs=VM, compiler_params=slots_params,
            scratch_shapes=[pltpu.VMEM((room.spread, classes, size), jnp.float32)],
            name="grads",
        )(*scalars, residual, tiles)
        grads = pl.pallas_call(
            functools.partial(gather_kernel, room, n_rows),
            out_shape=packed, in_specs=[VM], out_specs=VM, compiler_params=remote(1),
            scratch_shapes=[
                pltpu.VMEM((3, shared, classes, size), jnp.bfloat16),
                pltpu.VMEM((shared, classes, size), jnp.bfloat16),
                pltpu.VMEM((shared, classes, size), jnp.bfloat16),
                *remote_sems(11),
            ],
            name="gather",
        )(grads)
        shape = jax.ShapeDtypeStruct(current.shape, current.dtype)
        more = step + 1 < steps
        current, *send = pl.pallas_call(
            functools.partial(apply_pack_lists if more else apply_lists, room, step),
            out_shape=(shape, packed) if more else (shape,),
            in_specs=[SM, SM, VM, VM], out_specs=(VM, VM) if more else (VM,),
            compiler_params=LOCAL, name="apply",
        )(lists, learning_rate, current, grads)
        send = send[0] if more else None
    return current, jnp.concatenate(losses)


def team_device(
    tiles, tile_scales, tile_rows, tile_cols, tile_counts, labels, learning_rate, weights
):
    args = (tiles, tile_scales, tile_rows, tile_cols, tile_counts, labels, learning_rate, weights)
    size = tiles.shape[-1]
    n_rows, n_cols = lax.axis_size("rows"), lax.axis_size("cols")
    cols = tile_cols[:, 0, 0]
    counts = tile_counts[:, 0, 0]
    everyone, live = mark(cols, counts, n_rows, n_cols, size)
    code, lists, tier = plan(everyone, live, n_rows)
    args = (*args[:4], counts, *args[5:])
    branches = [
        functools.partial(team_program, n_rows, listed, shared, branch)
        for branch, (listed, shared) in enumerate((*TIERS, (size, size)))
    ]
    return lax.switch(tier[0], branches, code, lists, *args)


def either_device(*args):
    tiles, weights, labels = args[0], args[-1], args[5]
    n_rows, n_cols = lax.axis_size("rows"), lax.axis_size("cols")
    size, steps = tiles.shape[-1], tiles.shape[0]
    even = n_rows == 8 and steps * n_rows * 3 <= size and labels.shape[1] // n_cols % size == 0
    if even and size == 128 and weights.shape[1] == size * size:
        return team_device(*args)
    return per_device(*args)


def solution(mesh):
    return jax.shard_map(
        either_device,
        mesh=mesh,
        in_specs=(
            P(None, "rows", "cols", None, None, None),
            P(None, "rows", "cols", None),
            P(None, "rows", "cols", None),
            P(None, "rows", "cols", None),
            P(None, "rows", "cols"),
            P(None, "rows"),
            P(),
            P(None, ("cols", "rows")),
        ),
        out_specs=(P(None, ("cols", "rows")), P(None, ("rows", "cols"))),
        check_vma=False,
    )
```
